512 devices in a mesh: dp: 16 (over z_hi, x, core), seq: 32 (over z_lo, y).
Axes of the slice: x: 4, y: 4, z: 16 (z_hi: 2, z_lo: 8; z = z_hi * 8 + z_lo), core: 2. Of those that a mesh axis runs over, the one named last changes fastest.
Arguments:
- grad_out: bfloat16 [16, 64, 32768], P('dp', None, 'seq'), may hold values from -6 to 6
- gate: bfloat16 [16, 64, 32768], P('dp', None, 'seq'), may hold values from -6 to 6
- input_spectrum: float32 [16, 2, 64, 32768], P('dp', None, None, 'seq'), may hold values from -6 to 6
- filter_spectrum: float32 [2, 64, 32768], P(None, 'dp', 'seq'), may hold values from -6 to 6
Outputs:
- grad_input: bfloat16 [16, 64, 32768], P('dp', None, 'seq')
- grad_gate: bfloat16 [16, 64, 32768], P('dp', None, 'seq')
- grad_filter: float32 [2, 64, 32768], P(None, 'dp', 'seq')
The draws below stay inside these ranges and needn't reach their ends.
All inputs are finite; a program needn't handle non-finite values.
Results may differ from the reference program's by a relative error of at most 0.002.
Values sent between devices are 32-bit elements; how exact they have to be, the bound alone decides.
No kernel may reach another device: no remote copies, remote signals or barrier semaphores. Data moves between devices by JAX's collectives and lax.ppermute only.
A program may use at most 64 MiB of HBM per device.

```python
import jax
import jax.numpy as jnp
from jax import lax

CHANNELS = 64
POS_DEV = 1024
SEQ_LEN = 32768
BATCH = 16
N_SEQ = 32


def raised(result, own_key, source, target, parts, factor):
    owner, partner = [(jnp.arange(result.shape[axis_at]) // (result.shape[axis_at] // parts)).reshape([-1 if axis == axis_at else 1 for axis in range(result.ndim)]) for axis_at in (source, target)]
    chosen = jax.random.permutation(own_key, parts)[partner]
    strong = (owner == chosen) | (owner == (partner + parts // 2) % parts)
    return jnp.where(strong, factor * result, result)


def steps_of(own_key, extent, cuts, least, top_value):
    factor_of, own = 1.0, jax.random.fold_in(own_key, 6)
    for axis_at, parts in cuts:
        heights = jnp.exp(jax.random.uniform(jax.random.fold_in(own, axis_at), (parts,), jnp.float32, least / len(cuts), top_value / len(cuts)))
        factor_of = factor_of * jnp.repeat(heights, extent[axis_at] // parts).reshape([-1 if axis == axis_at else 1 for axis in range(len(extent))])
    return factor_of


def gaussian(stream_key, dims, scale, bound, pieces=(), dtype=jnp.bfloat16):
    factor_of = steps_of(stream_key, dims, pieces, -0.22, 0.18) if pieces else 1.0
    array = jax.random.normal(stream_key, dims, jnp.float32) * scale * factor_of
    return jnp.minimum(jnp.maximum(array, -bound), bound).astype(dtype)


def gaussian_with(own_key, dims, deviation, bound, cuts, heavy, held_as=jnp.bfloat16):
    array = deviation * jax.random.normal(own_key, dims, jnp.float32)
    if cuts:
        array = array * steps_of(own_key, dims, cuts, -0.22, 0.18)
    return jnp.clip(raised(array, jax.random.fold_in(own_key, 3), *heavy), -bound, bound).astype(held_as)


def setup_inputs(seed: int = 0) -> dict:
    streams_of = jax.random.split(jax.random.key(seed), 5)
    return {
        "grad_out": gaussian_with(streams_of[0], (BATCH, CHANNELS, SEQ_LEN), 1.0, 6.0, ((0, 16), (2, 32)), (0, 1, 16, 2.0)),
        "gate": gaussian(streams_of[1], (BATCH, CHANNELS, SEQ_LEN), 1.0, 6.0, ((0, 16), (2, 32))),
        "input_spectrum": gaussian(streams_of[2], (BATCH, 2, CHANNELS, SEQ_LEN), 1.0, 6.0, ((0, 16), (3, 32)), jnp.float32),
        "filter_spectrum": gaussian(streams_of[3], (2, CHANNELS, SEQ_LEN), 1.0, 6.0, ((1, 16), (2, 32)), jnp.float32),
    }


def natural_order(spectrum):
    shape = spectrum.shape
    return spectrum.reshape(shape[:-1] + (N_SEQ, POS_DEV)).swapaxes(-1, -2).reshape(shape)

def stored_order(spectrum):
    shape = spectrum.shape
    return spectrum.reshape(shape[:-1] + (POS_DEV, N_SEQ)).swapaxes(-1, -2).reshape(shape)

def reference(grad_out, gate, input_spectrum, filter_spectrum):
    root_len = jnp.sqrt(jnp.float32(SEQ_LEN))
    spec_in = natural_order(input_spectrum[:, 0]) + 1j * natural_order(input_spectrum[:, 1])
    spec_filt = natural_order(filter_spectrum[0]) + 1j * natural_order(filter_spectrum[1])
    conv = jnp.real(jnp.fft.ifft(spec_in * spec_filt, axis=-1)) * root_len
    upstream = grad_out.astype(jnp.float32)
    delta = upstream * gate.astype(jnp.float32)
    spec_delta = jnp.fft.fft(delta, axis=-1) / root_len
    grad_input = (jnp.real(jnp.fft.ifft(jnp.conj(spec_filt) * spec_delta, axis=-1)) * root_len).astype(jnp.bfloat16)
    grad_gate = (upstream * conv).astype(jnp.bfloat16)
    summed = lax.optimization_barrier(jnp.sum(jnp.conj(spec_in) * spec_delta, axis=0))
    grad_filter = jnp.stack([stored_order(jnp.real(summed)), stored_order(jnp.imag(summed))])
    return (grad_input, grad_gate, grad_filter)
```

```python
import math

import jax
import jax.numpy as jnp
import numpy as np
from jax import lax
from jax.experimental import pallas as pl
from jax.experimental.pallas import tpu as pltpu
from jax.sharding import Mesh, PartitionSpec as P


f32 = jnp.float32
bf16 = jnp.bfloat16
SEQ = ("zlo", "y")
DP = ("zhi", "x", "core")
MIB = 1024 * 1024


def unit_roots(rows, columns, period):
    product = np.outer(np.arange(rows, dtype=np.int64), np.arange(columns, dtype=np.int64))
    angle = (product % period).astype(np.float64) * (2.0 * np.pi / period)
    return np.cos(angle).astype(np.float32), np.sin(angle).astype(np.float32)


def halves(values):
    high = values.astype(bf16)
    return high, (values - high.astype(f32)).astype(bf16)


def dot_small(left, right):
    return jnp.dot(left, right, precision=lax.Precision.HIGHEST, preferred_element_type=f32)


def dot16(left, right):
    return jnp.dot(left, right, preferred_element_type=f32)


def tables_kernel(coarse_ref, fine_ref, cos_hi, cos_lo, sin_hi, sin_lo):
    steps = fine_ref.shape[1]

    @pl.loop(0, coarse_ref.shape[1])
    def _(a):
        at = pl.ds(pl.multiple_of(a * steps, steps), steps)
        coarse_cos, coarse_sin = coarse_ref[0, pl.ds(a, 1), :], coarse_ref[1, pl.ds(a, 1), :]
        fine_cos, fine_sin = fine_ref[0], fine_ref[1]
        cosine = coarse_cos * fine_cos - coarse_sin * fine_sin
        sine = coarse_sin * fine_cos + coarse_cos * fine_sin
        cos_hi[at, :], cos_lo[at, :] = halves(cosine)
        sin_hi[at, :], sin_lo[at, :] = halves(sine)


def root_tables(points):
    steps = 32
    coarse_cos, coarse_sin = unit_roots(points // steps, points, points // steps)
    fine_cos, fine_sin = unit_roots(steps, points, points)
    coarse = jnp.asarray(np.stack([coarse_cos, coarse_sin]))
    fine = jnp.asarray(np.stack([fine_cos, fine_sin]))
    return pl.pallas_call(
        tables_kernel,
        out_shape=[jax.ShapeDtypeStruct((points, points), bf16)] * 4,
        name="root_tables",
        compiler_params=pltpu.CompilerParams(vmem_limit_bytes=24 * MIB),
        cost_estimate=pl.CostEstimate(
            flops=20 * points * points, bytes_accessed=8 * points * points, transcendentals=0
        ),
    )(coarse, fine)


def root_product(high_low, rows, hi_ref, lo_ref, at):
    both = dot16(high_low, hi_ref[:, at])
    return both[:rows] + both[rows:] + dot16(high_low[:rows], lo_ref[:, at])


def forward_kernel(
    moved_ref, small_ref, twiddle_ref, cos_hi, cos_lo, sin_hi, sin_lo, spec_ref, terms_ref, rows_ref
):
    classes = moved_ref.shape[0]
    points = cos_hi.shape[0]
    scale = 1.0 / math.sqrt(classes * points)
    tw_cos, tw_sin = twiddle_ref[0], twiddle_ref[1]
    for channel in range(2):
        delta = moved_ref[:, (4 + channel) * points : (5 + channel) * points]
        part_real = dot_small(small_ref[0], delta)
        part_imag = -dot_small(small_ref[1], delta)
        turned_real = part_real * tw_cos + part_imag * tw_sin
        turned_imag = part_imag * tw_cos - part_real * tw_sin
        for place, turned in ((channel, turned_real), (2 + channel, turned_imag)):
            high, low = halves(turned * scale)
            rows_ref[place * classes : (place + 1) * classes, :] = high
            rows_ref[(4 + place) * classes : (5 + place) * classes, :] = low
    half = 2 * classes
    for tile in range(4):
        width = points // 4
        at = slice(tile * width, (tile + 1) * width)
        by_cos = root_product(rows_ref[...], 4 * classes, cos_hi, cos_lo, at)
        by_sin = root_product(rows_ref[...], 4 * classes, sin_hi, sin_lo, at)
        real = by_cos[:half] + by_sin[half:]
        imag = by_cos[half:] - by_sin[:half]
        for channel in range(2):
            mine = slice(channel * classes, (channel + 1) * classes)
            put_real = slice(channel * points + at.start, channel * points + at.stop)
            put_imag = slice((2 + channel) * points + at.start, (2 + channel) * points + at.stop)
            in_real, in_imag = moved_ref[:, put_real], moved_ref[:, put_imag]
            spec_ref[:, put_real] = real[mine]
            spec_ref[:, put_imag] = imag[mine]
            terms_ref[:, put_real] = in_real * real[mine] + in_imag * imag[mine]
            terms_ref[:, put_imag] = in_real * imag[mine] - in_imag * real[mine]


def inverse_kernel(
    moved_ref, filt_ref, spec_ref, small_ref, twiddle_ref, cos_hi, cos_lo, sin_hi, sin_lo, out_ref,
    rows_ref,
):
    classes = moved_ref.shape[0]
    points = cos_hi.shape[0]

    def keep(place, values):
        high, low = halves(values)
        rows_ref[place * classes : (place + 1) * classes, :] = high
        rows_ref[(8 + place) * classes : (9 + place) * classes, :] = low

    for channel in range(2):
        real_at = slice(channel * points, (channel + 1) * points)
        imag_at = slice((2 + channel) * points, (3 + channel) * points)
        filt_real, filt_imag = filt_ref[:, real_at], filt_ref[:, imag_at]
        in_real, in_imag = moved_ref[:, real_at], moved_ref[:, imag_at]
        keep(channel, in_real * filt_real - in_imag * filt_imag)
        keep(4 + channel, in_real * filt_imag + in_imag * filt_real)
        delta_real, delta_imag = spec_ref[:, real_at], spec_ref[:, imag_at]
        keep(2 + channel, filt_real * delta_real + filt_imag * delta_imag)
        keep(6 + channel, filt_real * delta_imag - filt_imag * delta_real)
    half = 4 * classes
    for tile in range(4):
        width = points // 4
        at = slice(tile * width, (tile + 1) * width)
        by_cos = root_product(rows_ref[...], 8 * classes, cos_hi, cos_lo, at)
        by_sin = root_product(rows_ref[...], 8 * classes, sin_hi, sin_lo, at)
        real = by_cos[:half] - by_sin[half:]
        imag = by_cos[half:] + by_sin[:half]
        tw_cos, tw_sin = twiddle_ref[0, :, at], twiddle_ref[1, :, at]
        for place in range(4):
            mine = slice(place * classes, (place + 1) * classes)
            turned_real = real[mine] * tw_cos - imag[mine] * tw_sin
            turned_imag = imag[mine] * tw_cos + real[mine] * tw_sin
            out_ref[:, place * points + at.start : place * points + at.stop] = dot_small(
                small_ref[0], turned_real
            ) - dot_small(small_ref[1], turned_imag)


def staging_pairs(shape):
    zhi_count, group_count, seq_count = shape
    pairs = []
    for zhi_shift in range(2):
        for half_shift in range(2):
            found = []
            for d in range(zhi_count * group_count):
                for s in range(seq_count):
                    half = (half_shift + s) % 2
                    zhi = (zhi_shift + s // 2) % 2
                    target = (zhi * group_count + s // 4) * seq_count + 2 * d + half
                    found.append((d * seq_count + s, target))
            pairs.append(found)
    return pairs


def per_device(grad_out, gate, input_spectrum, filter_spectrum):
    _, channels, positions = grad_out.shape
    seq_count = lax.axis_size(SEQ)
    everyone = DP + SEQ
    seq_index = lax.axis_index(SEQ)
    zhi_index = lax.axis_index("zhi")
    core_index = lax.axis_index("core")
    x_index = lax.axis_index("x")
    x_count = lax.axis_size("x")
    odd = seq_index % 2 == 1
    pairs = staging_pairs((lax.axis_size("zhi"), x_count * 2, seq_count))
    per_seq = channels // seq_count

    upstream = grad_out.astype(f32)
    delta = (upstream * gate.astype(f32)).reshape(seq_count, per_seq * positions)
    spectrum = (
        input_spectrum.reshape(2, seq_count, per_seq, positions)
        .transpose(1, 0, 2, 3)
        .reshape(seq_count, 2 * per_seq * positions)
    )
    with jax.named_scope("gather_seq"):
        moved = lax.all_to_all(
            jnp.concatenate([spectrum, delta], axis=1), SEQ, split_axis=0, concat_axis=0, tiled=True
        )

    low_half, high_half = filter_spectrum[:, :2], filter_spectrum[:, 2:]
    sent = [jnp.where(odd, high_half, low_half), jnp.where(odd, low_half, high_half)]
    with jax.named_scope("stage_filter"):
        got = [
            lax.ppermute(sent[number % 2], everyone, pairs[number]).reshape(1, 4 * positions)
            for number in range(4)
        ]
    upper = zhi_index == 1
    got = [jnp.where(upper, got[n ^ 2], got[n]) for n in range(4)]
    got = [jnp.where(odd, got[n ^ 1], got[n]) for n in range(4)]
    with jax.named_scope("gather_filter"):
        filters = lax.all_gather(jnp.concatenate(got, axis=0), ("x", "core"), axis=0, tiled=True)

    with jax.named_scope("tables"):
        tables = root_tables(positions)
    small = jnp.asarray(np.stack(unit_roots(seq_count, seq_count, seq_count)))
    twiddle = jnp.asarray(np.stack(unit_roots(seq_count, positions, seq_count * positions)))

    wide = jax.ShapeDtypeStruct((seq_count, 4 * positions), f32)
    params = pltpu.CompilerParams(vmem_limit_bytes=40 * MIB)
    with jax.named_scope("forward"):
        spec, terms = pl.pallas_call(
            forward_kernel,
            out_shape=[wide, wide],
            scratch_shapes=[pltpu.VMEM((8 * seq_count, positions), bf16)],
            name="forward",
            compiler_params=params,
            cost_estimate=pl.CostEstimate(flops=2 * 10**9, bytes_accessed=10**7, transcendentals=0),
        )(moved, small, twiddle, *tables)

    with jax.named_scope("sum_core"):
        parts = terms.reshape(x_count, 2, 4, 4 * positions)
        first = core_index == 0
        kept = jnp.where(first, parts[:, 0], parts[:, 1])
        away = jnp.where(first, parts[:, 1], parts[:, 0])
        summed = kept + lax.ppermute(away, "core", [(0, 1), (1, 0)])
    with jax.named_scope("sum_x"):
        total = lax.dynamic_index_in_dim(summed, x_index, 0, keepdims=False)
        for shift in range(1, x_count):
            away = lax.dynamic_index_in_dim(summed, (x_index + shift) % x_count, 0, keepdims=False)
            total = total + lax.ppermute(
                away, "x", [(x, (x + shift) % x_count) for x in range(x_count)]
            )

    with jax.named_scope("inverse"):
        signals = pl.pallas_call(
            inverse_kernel,
            out_shape=wide,
            scratch_shapes=[pltpu.VMEM((16 * seq_count, positions), bf16)],
            name="inverse",
            compiler_params=params,
            cost_estimate=pl.CostEstimate(flops=4 * 10**9, bytes_accessed=10**7, transcendentals=0),
        )(moved, filters, spec, small, twiddle, *tables)
    with jax.named_scope("scatter_seq"):
        returned = lax.all_to_all(signals, SEQ, split_axis=0, concat_axis=0, tiled=True)

    pieces = [total[n] for n in range(4)]
    pieces = [jnp.where(upper, pieces[n ^ 2], pieces[n]) for n in range(4)]
    pieces = [jnp.where(odd, pieces[n ^ 1], pieces[n]) for n in range(4)]
    with jax.named_scope("return_filter"):
        back = [
            lax.ppermute(pieces[number], everyone, [(b, a) for a, b in pairs[number]])
            for number in range(4)
        ]
    even_half = (back[0] + back[2]).reshape(2, per_seq, positions)
    odd_half = (back[1] + back[3]).reshape(2, per_seq, positions)
    grad_filter = jnp.concatenate(
        [jnp.where(odd, odd_half, even_half), jnp.where(odd, even_half, odd_half)], axis=1
    )

    scale = 1.0 / math.sqrt(seq_count * positions)
    conv = returned[:, : per_seq * positions].reshape(1, channels, positions) * scale
    backward = returned[:, per_seq * positions :].reshape(1, channels, positions) * scale
    grad_gate = (upstream * conv).astype(bf16)
    return (backward.astype(bf16), grad_gate, grad_filter)


def solution(mesh):
    split = Mesh(mesh.devices.reshape(2, 4, 2, 8, 4), DP + SEQ)
    return jax.shard_map(
        per_device,
        mesh=split,
        in_specs=(P(DP, None, SEQ), P(DP, None, SEQ), P(DP, None, None, SEQ), P(None, DP, SEQ)),
        out_specs=(P(DP, None, SEQ), P(DP, None, SEQ), P(None, DP, SEQ)),
        check_vma=False,
    )
```

```python
import functools
import math

import jax
import jax.numpy as jnp
import numpy as np
from jax import lax
from jax.experimental import pallas as pl
from jax.experimental.pallas import tpu as pltpu
from jax.sharding import Mesh, PartitionSpec as P


f32 = jnp.float32
bf16 = jnp.bfloat16
SEQ = ("zlo", "y")
DP = ("zhi", "x", "core")
MIB = 1024 * 1024


def unit_roots(rows, columns, period):
    product = np.outer(np.arange(rows, dtype=np.int64), np.arange(columns, dtype=np.int64))
    angle = (product % period).astype(np.float64) * (2.0 * np.pi / period)
    return np.cos(angle).astype(np.float32), np.sin(angle).astype(np.float32)


def halves(values):
    high = values.astype(bf16)
    return high, (values - high.astype(f32)).astype(bf16)


def three_terms(values, axis):
    high, low = halves(values)
    return jnp.concatenate([high, low, high], axis=axis)


def small_table(points, inverse):
    cosine, sine = unit_roots(points, points, points)
    whole = np.concatenate([cosine, -sine], axis=1 if inverse else 0)
    high = whole.astype(bf16)
    low = (whole - high.astype(np.float32)).astype(bf16)
    return jnp.asarray(np.concatenate([high, high, low], axis=1))


def dot16(left, right):
    return jnp.dot(left, right, preferred_element_type=f32)


def tables_kernel(coarse_ref, fine_ref, cos_hi, cos_lo, sin_hi, sin_lo):
    steps = fine_ref.shape[1]

    @pl.loop(0, coarse_ref.shape[1])
    def _(a):
        at = pl.ds(pl.multiple_of(a * steps, steps), steps)
        coarse_cos, coarse_sin = coarse_ref[0, pl.ds(a, 1), :], coarse_ref[1, pl.ds(a, 1), :]
        fine_cos, fine_sin = fine_ref[0], fine_ref[1]
        cosine = coarse_cos * fine_cos - coarse_sin * fine_sin
        sine = coarse_sin * fine_cos + coarse_cos * fine_sin
        cos_hi[at, :], cos_lo[at, :] = halves(cosine)
        sin_hi[at, :], sin_lo[at, :] = halves(sine)


def root_tables(points):
    steps, columns = 32, points // 4
    coarse = jnp.asarray(np.stack(unit_roots(points // steps, columns, points // steps)))
    fine = jnp.asarray(np.stack(unit_roots(steps, columns, points)))
    return pl.pallas_call(
        tables_kernel,
        out_shape=[jax.ShapeDtypeStruct((points, columns), bf16)] * 4,
        name="root_tables",
        compiler_params=pltpu.CompilerParams(vmem_limit_bytes=16 * MIB),
        cost_estimate=pl.CostEstimate(
            flops=20 * points * columns, bytes_accessed=8 * points * columns, transcendentals=0
        ),
    )(coarse, fine)


def keep_quarters(rows_ref, place, count, real, imag, conjugate):
    rows, points = real.shape
    lane = lax.broadcasted_iota(jnp.int32, (1, points), 1)
    odd = lane % 2 == 1
    alternate = jnp.where(odd, -1.0, 1.0)
    early = jnp.where(lane % 4 < 2, 1.0, -1.0)
    outer = jnp.where((lane + 1) % 4 < 2, 1.0, -1.0)
    swap_real, swap_imag = jnp.where(odd, imag, real), jnp.where(odd, real, imag)
    turned = [
        (real, imag),
        (swap_real * outer, swap_imag * early),
        (real * alternate, imag * alternate),
        (swap_real * early, swap_imag * outer),
    ]
    if conjugate:
        turned[1], turned[3] = turned[3], turned[1]
    for m in range(4):
        for part, values in enumerate(turned[m]):
            high, low = halves(values)
            first = (part * count + place) * rows
            rows_ref[m, first : first + rows, :] = high
            rows_ref[m, 2 * count * rows + first : 2 * count * rows + first + rows, :] = low


def root_product(high_low, hi_ref, lo_ref):
    rows = high_low.shape[0] // 2
    both = dot16(high_low, hi_ref[...])
    return both[:rows] + both[rows:] + dot16(high_low[:rows], lo_ref[...])


def forward_kernel(
    moved_ref, small_ref, twiddle_ref, cos_hi, cos_lo, sin_hi, sin_lo, spec_ref, terms_ref, rows_ref
):
    classes = moved_ref.shape[0]
    points = cos_hi.shape[0]
    scale = 1.0 / math.sqrt(classes * points)
    tw_cos, tw_sin = twiddle_ref[0] * scale, twiddle_ref[1] * scale
    for channel in range(2):
        delta = moved_ref[:, (4 + channel) * points : (5 + channel) * points]
        part = dot16(small_ref[...], three_terms(delta, 0))
        part_real, part_imag = part[:classes], part[classes:]
        turned_real = part_real * tw_cos + part_imag * tw_sin
        turned_imag = part_imag * tw_cos - part_real * tw_sin
        keep_quarters(rows_ref, channel, 2, turned_real, turned_imag, True)
    half = 2 * classes
    width = points // 4
    for tile in range(4):
        at = slice(tile * width, (tile + 1) * width)
        by_cos = root_product(rows_ref[tile], cos_hi, cos_lo)
        by_sin = root_product(rows_ref[tile], sin_hi, sin_lo)
        real = by_cos[:half] + by_sin[half:]
        imag = by_cos[half:] - by_sin[:half]
        for channel in range(2):
            mine = slice(channel * classes, (channel + 1) * classes)
            put_real = slice(channel * points + at.start, channel * points + at.stop)
            put_imag = slice((2 + channel) * points + at.start, (2 + channel) * points + at.stop)
            in_real, in_imag = moved_ref[:, put_real], moved_ref[:, put_imag]
            spec_ref[:, put_real] = real[mine]
            spec_ref[:, put_imag] = imag[mine]
            terms_ref[:, put_real] = in_real * real[mine] + in_imag * imag[mine]
            terms_ref[:, put_imag] = in_real * imag[mine] - in_imag * real[mine]


def inverse_kernel(
    sign, first_ref, filt_ref, small_ref, twiddle_ref, cos_hi, cos_lo, sin_hi, sin_lo, out_ref,
    rows_ref,
):
    classes = first_ref.shape[0]
    points = cos_hi.shape[0]

    for channel in range(2):
        real_at = slice(channel * points, (channel + 1) * points)
        imag_at = slice((2 + channel) * points, (3 + channel) * points)
        filt_real, filt_imag = filt_ref[:, real_at], filt_ref[:, imag_at] * sign
        first_real, first_imag = first_ref[:, real_at], first_ref[:, imag_at]
        keep_quarters(
            rows_ref,
            channel,
            2,
            first_real * filt_real - first_imag * filt_imag,
            first_real * filt_imag + first_imag * filt_real,
            False,
        )
    half = 2 * classes
    width = points // 4
    for tile in range(4):
        at = slice(tile * width, (tile + 1) * width)
        by_cos = root_product(rows_ref[tile], cos_hi, cos_lo)
        by_sin = root_product(rows_ref[tile], sin_hi, sin_lo)
        real = by_cos[:half] - by_sin[half:]
        imag = by_cos[half:] + by_sin[:half]
        tw_cos, tw_sin = twiddle_ref[0, :, at], twiddle_ref[1, :, at]
        for channel in range(2):
            mine = slice(channel * classes, (channel + 1) * classes)
            turned = jnp.concatenate(
                [
                    real[mine] * tw_cos - imag[mine] * tw_sin,
                    imag[mine] * tw_cos + real[mine] * tw_sin,
                ],
                axis=0,
            )
            out_ref[:, channel * points + at.start : channel * points + at.stop] = dot16(
                small_ref[...], three_terms(turned, 0)
            )


def staging_pairs(x_count, core_count, seq_count):
    per_core, per_x = seq_count // core_count, seq_count // (core_count * x_count)
    pairs = []
    for number in range(2):
        found = []
        for d in range(2 * x_count * core_count):
            for s in range(seq_count):
                core, x, zhi = s // per_core, s % per_core // per_x, s % per_x // 2
                row = (zhi * x_count + x) * core_count + core
                found.append((d * seq_count + s, row * seq_count + 2 * d + ((s % 2) ^ number)))
        pairs.append(found)
    return pairs


def halving(values, upper, axis, pairs):
    rows = values.shape[0] // 2
    kept = jnp.where(upper, values[rows:], values[:rows])
    away = jnp.where(upper, values[:rows], values[rows:])
    return kept + lax.ppermute(away, axis, pairs)


def step(grad_out, gate, input_spectrum, filter_spectrum):
    _, channels, positions = grad_out.shape
    seq_count = lax.axis_size(SEQ)
    x_count = lax.axis_size("x")
    everyone = DP + SEQ
    odd = lax.axis_index(SEQ) % 2 == 1
    upper_zhi = lax.axis_index("zhi") == 1
    upper_core = lax.axis_index("core") == 1
    x_index = lax.axis_index("x")
    pairs = staging_pairs(x_count, 2, seq_count)
    per_seq = channels // seq_count

    upstream = grad_out.astype(f32)
    delta = (upstream * gate.astype(f32)).reshape(seq_count, per_seq * positions)
    spectrum = (
        input_spectrum.reshape(2, seq_count, per_seq, positions)
        .transpose(1, 0, 2, 3)
        .reshape(seq_count, 2 * per_seq * positions)
    )
    moved = lax.all_to_all(
        jnp.concatenate([spectrum, delta], axis=1), SEQ, split_axis=0, concat_axis=0, tiled=True
    )

    low_half, high_half = filter_spectrum[:, :2], filter_spectrum[:, 2:]
    sent = [jnp.where(odd, high_half, low_half), jnp.where(odd, low_half, high_half)]
    got = [
        lax.ppermute(sent[number], everyone, pairs[number]).reshape(1, 4 * positions)
        for number in range(2)
    ]
    pair = jnp.concatenate(
        [jnp.where(odd, got[1], got[0]), jnp.where(odd, got[0], got[1])], axis=0
    )
    other = lax.ppermute(pair, "zhi", [(0, 1), (1, 0)])
    four = jnp.concatenate(
        [jnp.where(upper_zhi, other, pair), jnp.where(upper_zhi, pair, other)], axis=0
    )
    filters = lax.all_gather(four, ("core", "x"), axis=0, tiled=True)

    tables = root_tables(positions)
    small_out = small_table(seq_count, False)
    small_back = small_table(seq_count, True)
    twiddle = jnp.asarray(np.stack(unit_roots(seq_count, positions, seq_count * positions)))

    wide = jax.ShapeDtypeStruct((seq_count, 4 * positions), f32)
    signal = jax.ShapeDtypeStruct((seq_count, 2 * positions), f32)
    rows = [pltpu.VMEM((4, 8 * seq_count, positions), bf16)]
    params = pltpu.CompilerParams(vmem_limit_bytes=16 * MIB)
    cost = pl.CostEstimate(flops=2 * 10**9, bytes_accessed=10**7, transcendentals=0)
    spec, terms = pl.pallas_call(
        forward_kernel,
        out_shape=[wide, wide],
        scratch_shapes=rows,
        name="forward",
        compiler_params=params,
        cost_estimate=cost,
    )(moved, small_out, twiddle, *tables)

    def inverse(sign, first):
        return pl.pallas_call(
            functools.partial(inverse_kernel, sign),
            out_shape=signal,
            scratch_shapes=rows,
            name="inverse",
            compiler_params=params,
            cost_estimate=cost,
        )(first, filters, small_back, twiddle, *tables)

    total = halving(terms, upper_core, "core", [(0, 1), (1, 0)])
    total = halving(total, x_index >= 2, "x", [(x, x ^ 2) for x in range(x_count)])
    total = halving(total, x_index % 2 == 1, "x", [(x, x ^ 1) for x in range(x_count)])
    total = halving(total, upper_zhi, "zhi", [(0, 1), (1, 0)])

    conv = inverse(1.0, moved)
    back = inverse(-1.0, spec)
    returned = lax.all_to_all(
        jnp.concatenate([conv, back], axis=1), SEQ, split_axis=0, concat_axis=0, tiled=True
    )

    pieces = [total[0], total[1]]
    pieces = [jnp.where(odd, pieces[1 - n], pieces[n]) for n in range(2)]
    ends = [
        lax.ppermute(pieces[number], everyone, [(b, a) for a, b in pairs[number]]).reshape(
            2, per_seq, positions
        )
        for number in range(2)
    ]
    grad_filter = jnp.concatenate(
        [jnp.where(odd, ends[1], ends[0]), jnp.where(odd, ends[0], ends[1])], axis=1
    )

    scale = 1.0 / math.sqrt(seq_count * positions)
    conv = returned[:, : per_seq * positions].reshape(1, channels, positions) * scale
    backward = returned[:, per_seq * positions :].reshape(1, channels, positions) * scale
    grad_gate = (upstream * conv).astype(bf16)
    return (backward.astype(bf16), grad_gate, grad_filter)


def solution(mesh):
    split = Mesh(mesh.devices.reshape(2, 4, 2, 8, 4), DP + SEQ)
    return jax.shard_map(
        step,
        mesh=split,
        in_specs=(P(DP, None, SEQ), P(DP, None, SEQ), P(DP, None, None, SEQ), P(None, DP, SEQ)),
        out_specs=(P(DP, None, SEQ), P(DP, None, SEQ), P(None, DP, SEQ)),
        check_vma=False,
    )
```

```python
import functools
import math

import jax
import jax.numpy as jnp
import numpy as np
from jax import lax
from jax.experimental import pallas as pl
from jax.experimental.pallas import tpu as pltpu
from jax.sharding import Mesh, PartitionSpec as P


f32 = jnp.float32
bf16 = jnp.bfloat16
SEQ = ("zlo", "y")
DP = ("zhi", "x", "core")
MIB = 1024 * 1024


def unit_roots(rows, columns, period):
    product = np.outer(np.arange(rows, dtype=np.int64), np.arange(columns, dtype=np.int64))
    angle = (product % period).astype(np.float64) * (2.0 * np.pi / period)
    return np.cos(angle).astype(np.float32), np.sin(angle).astype(np.float32)


def halves(values):
    high = values.astype(bf16)
    return high, (values - high.astype(f32)).astype(bf16)


def three_terms(values, axis):
    high, low = halves(values)
    return jnp.concatenate([high, low, high], axis=axis)


def small_table(points, inverse):
    cosine, sine = unit_roots(points, points, points)
    whole = np.concatenate([cosine, -sine], axis=1 if inverse else 0)
    high = whole.astype(bf16)
    low = (whole - high.astype(np.float32)).astype(bf16)
    return jnp.asarray(np.concatenate([high, high, low], axis=1))


def dot16(left, right):
    return jnp.dot(left, right, preferred_element_type=f32)


def tables_kernel(coarse_ref, fine_ref, cos_hi, cos_lo, sin_hi, sin_lo):
    steps = fine_ref.shape[1]

    @pl.loop(0, coarse_ref.shape[1])
    def _(a):
        at = pl.ds(pl.multiple_of(a * steps, steps), steps)
        coarse_cos, coarse_sin = coarse_ref[0, pl.ds(a, 1), :], coarse_ref[1, pl.ds(a, 1), :]
        fine_cos, fine_sin = fine_ref[0], fine_ref[1]
        cosine = coarse_cos * fine_cos - coarse_sin * fine_sin
        sine = coarse_sin * fine_cos + coarse_cos * fine_sin
        cos_hi[at, :], cos_lo[at, :] = halves(cosine)
        sin_hi[at, :], sin_lo[at, :] = halves(sine)


def root_tables(points):
    steps, columns = 32, points // 4
    coarse = jnp.asarray(np.stack(unit_roots(points // steps, columns, points // steps)))
    fine = jnp.asarray(np.stack(unit_roots(steps, columns, points)))
    return pl.pallas_call(
        tables_kernel,
        out_shape=[jax.ShapeDtypeStruct((points, columns), bf16)] * 4,
        name="root_tables",
        compiler_params=pltpu.CompilerParams(vmem_limit_bytes=16 * MIB),
        cost_estimate=pl.CostEstimate(
            flops=20 * points * columns, bytes_accessed=8 * points * columns, transcendentals=0
        ),
    )(coarse, fine)


def keep_quarters(rows_ref, place, count, real, imag, conjugate):
    rows, points = real.shape
    lane = lax.broadcasted_iota(jnp.int32, (1, points), 1)
    odd = lane % 2 == 1
    alternate = jnp.where(odd, -1.0, 1.0)
    early = jnp.where(lane % 4 < 2, 1.0, -1.0)
    outer = jnp.where((lane + 1) % 4 < 2, 1.0, -1.0)
    swap_real, swap_imag = jnp.where(odd, imag, real), jnp.where(odd, real, imag)
    turned = [
        (real, imag),
        (swap_real * outer, swap_imag * early),
        (real * alternate, imag * alternate),
        (swap_real * early, swap_imag * outer),
    ]
    if conjugate:
        turned[1], turned[3] = turned[3], turned[1]
    for m in range(4):
        for part, values in enumerate(turned[m]):
            high, low = halves(values)
            first = (part * count + place) * rows
            rows_ref[m, first : first + rows, :] = high
            rows_ref[m, 2 * count * rows + first : 2 * count * rows + first + rows, :] = low


def root_product(high_low, hi_ref, lo_ref):
    rows = high_low.shape[0] // 2
    both = dot16(high_low, hi_ref[...])
    return both[:rows] + both[rows:] + dot16(high_low[:rows], lo_ref[...])


def forward_kernel(
    moved_ref, small_ref, twiddle_ref, cos_hi, cos_lo, sin_hi, sin_lo, spec_ref, terms_ref, rows_ref
):
    classes = moved_ref.shape[0]
    points = cos_hi.shape[0]
    scale = 1.0 / math.sqrt(classes * points)
    tw_cos, tw_sin = twiddle_ref[0] * scale, twiddle_ref[1] * scale
    for channel in range(2):
        delta = moved_ref[:, (4 + channel) * points : (5 + channel) * points]
        part = dot16(small_ref[...], three_terms(delta, 0))
        part_real, part_imag = part[:classes], part[classes:]
        turned_real = part_real * tw_cos + part_imag * tw_sin
        turned_imag = part_imag * tw_cos - part_real * tw_sin
        keep_quarters(rows_ref, channel, 2, turned_real, turned_imag, True)
    half = 2 * classes
    width = points // 4
    for tile in range(4):
        at = slice(tile * width, (tile + 1) * width)
        by_cos = root_product(rows_ref[tile], cos_hi, cos_lo)
        by_sin = root_product(rows_ref[tile], sin_hi, sin_lo)
        real = by_cos[:half] + by_sin[half:]
        imag = by_cos[half:] - by_sin[:half]
        for channel in range(2):
            mine = slice(channel * classes, (channel + 1) * classes)
            put_real = slice(channel * points + at.start, channel * points + at.stop)
            put_imag = slice((2 + channel) * points + at.start, (2 + channel) * points + at.stop)
            in_real, in_imag = moved_ref[:, put_real], moved_ref[:, put_imag]
            spec_ref[:, put_real] = real[mine]
            spec_ref[:, put_imag] = imag[mine]
            terms_ref[:, put_real] = in_real * real[mine] + in_imag * imag[mine]
            terms_ref[:, put_imag] = in_real * imag[mine] - in_imag * real[mine]


def inverse_kernel(
    sign, first_ref, filt_ref, small_ref, twiddle_ref, cos_hi, cos_lo, sin_hi, sin_lo, out_ref,
    rows_ref, turned_ref,
):
    classes = first_ref.shape[0]
    points = cos_hi.shape[0]

    for channel in range(2):
        real_at = slice(channel * points, (channel + 1) * points)
        imag_at = slice((2 + channel) * points, (3 + channel) * points)
        filt_real, filt_imag = filt_ref[:, real_at], filt_ref[:, imag_at] * sign
        first_real, first_imag = first_ref[:, real_at], first_ref[:, imag_at]
        keep_quarters(
            rows_ref,
            channel,
            2,
            first_real * filt_real - first_imag * filt_imag,
            first_real * filt_imag + first_imag * filt_real,
            False,
        )
    half = 2 * classes
    width = points // 4
    for tile in range(4):
        at = slice(tile * width, (tile + 1) * width)
        by_cos = root_product(rows_ref[tile], cos_hi, cos_lo)
        by_sin = root_product(rows_ref[tile], sin_hi, sin_lo)
        real = by_cos[:half] - by_sin[half:]
        imag = by_cos[half:] + by_sin[:half]
        tw_cos, tw_sin = twiddle_ref[0, :, at], twiddle_ref[1, :, at]
        for channel in range(2):
            mine = slice(channel * classes, (channel + 1) * classes)
            put = slice(channel * points + at.start, channel * points + at.stop)
            for part, turned in (
                (0, real[mine] * tw_cos - imag[mine] * tw_sin),
                (1, imag[mine] * tw_cos + real[mine] * tw_sin),
            ):
                high, low = halves(turned)
                for place, values in ((part, high), (2 + part, low), (4 + part, high)):
                    turned_ref[place * classes : (place + 1) * classes, put] = values
    out_ref[...] = dot16(small_ref[...], turned_ref[...])


def staging_pairs(x_count, core_count, seq_count):
    per_core, per_x = seq_count // core_count, seq_count // (core_count * x_count)
    pairs = []
    for number in range(2):
        found = []
        for d in range(2 * x_count * core_count):
            for s in range(seq_count):
                core, x, zhi = s // per_core, s % per_core // per_x, (s % per_x // 2) ^ number
                row = (zhi * x_count + x) * core_count + core
                found.append((d * seq_count + s, row * seq_count + 2 * d + s % 2))
        pairs.append(found)
    return pairs


def halving(values, upper, axis, pairs):
    rows = values.shape[0] // 2
    kept = jnp.where(upper, values[rows:], values[:rows])
    away = jnp.where(upper, values[:rows], values[rows:])
    return kept + lax.ppermute(away, axis, pairs)


def doubling(values, upper, axis, pairs):
    other = lax.ppermute(values, axis, pairs)
    return jnp.concatenate(
        [jnp.where(upper, other, values), jnp.where(upper, values, other)], axis=0
    )


def step(grad_out, gate, input_spectrum, filter_spectrum):
    _, channels, positions = grad_out.shape
    seq_count = lax.axis_size(SEQ)
    x_count = lax.axis_size("x")
    everyone = DP + SEQ
    odd = lax.axis_index(SEQ) % 2 == 1
    upper_zhi = lax.axis_index("zhi") == 1
    upper_core = lax.axis_index("core") == 1
    x_index = lax.axis_index("x")
    pairs = staging_pairs(x_count, 2, seq_count)
    per_seq = channels // seq_count

    upstream = grad_out.astype(f32)
    delta = (upstream * gate.astype(f32)).reshape(seq_count, per_seq * positions)
    spectrum = (
        input_spectrum.reshape(2, seq_count, per_seq, positions)
        .transpose(1, 0, 2, 3)
        .reshape(seq_count, 2 * per_seq * positions)
    )
    moved = lax.all_to_all(
        jnp.concatenate([spectrum, delta], axis=1), SEQ, split_axis=0, concat_axis=0, tiled=True
    )

    near_x = [(x, x ^ 1) for x in range(x_count)]
    far_x = [(x, x ^ 2) for x in range(x_count)]
    near_y = [(y, y ^ 1) for y in range(lax.axis_size("y"))]
    cores = [(0, 1), (1, 0)]
    wide_row = 4 * positions
    halves_of = filter_spectrum.reshape(2, 2, per_seq, positions).transpose(1, 0, 2, 3)
    sent = halves_of.reshape(2, wide_row)
    got = [lax.ppermute(sent, everyone, pairs[number]) for number in range(2)]
    first, second = jnp.where(upper_zhi, got[1], got[0]), jnp.where(upper_zhi, got[0], got[1])
    mine = jnp.stack([jnp.where(odd, v[1], v[0]) for v in (first, second)])
    away = jnp.stack([jnp.where(odd, v[0], v[1]) for v in (first, second)])
    other = lax.ppermute(away, "y", near_y)
    low, high = jnp.where(odd, other, mine), jnp.where(odd, mine, other)
    four = jnp.stack([low[0], high[0], low[1], high[1]])
    filters = doubling(four, x_index % 2 == 1, "x", near_x)
    filters = doubling(filters, x_index >= 2, "x", far_x)
    filters = doubling(filters, upper_core, "core", cores)

    tables = root_tables(positions)
    small_out = small_table(seq_count, False)
    small_back = small_table(seq_count, True)
    twiddle = jnp.asarray(np.stack(unit_roots(seq_count, positions, seq_count * positions)))

    wide = jax.ShapeDtypeStruct((seq_count, 4 * positions), f32)
    signal = jax.ShapeDtypeStruct((seq_count, 2 * positions), f32)
    rows = [pltpu.VMEM((4, 8 * seq_count, positions), bf16)]
    params = pltpu.CompilerParams(vmem_limit_bytes=16 * MIB)
    cost = pl.CostEstimate(flops=2 * 10**9, bytes_accessed=10**7, transcendentals=0)
    spec, terms = pl.pallas_call(
        forward_kernel,
        out_shape=[wide, wide],
        scratch_shapes=rows,
        name="forward",
        compiler_params=params,
        cost_estimate=cost,
    )(moved, small_out, twiddle, *tables)

    def inverse(sign, first):
        return pl.pallas_call(
            functools.partial(inverse_kernel, sign),
            out_shape=signal,
            scratch_shapes=rows + [pltpu.VMEM((6 * seq_count, 2 * positions), bf16)],
            name="inverse",
            compiler_params=params,
            cost_estimate=cost,
        )(first, filters, small_back, twiddle, *tables)

    total = halving(terms, upper_core, "core", cores)
    total = halving(total, x_index >= 2, "x", far_x)
    total = halving(total, x_index % 2 == 1, "x", near_x)
    mine = jnp.stack([jnp.where(odd, total[2 * n + 1], total[2 * n]) for n in range(2)])
    away = jnp.stack([jnp.where(odd, total[2 * n], total[2 * n + 1]) for n in range(2)])
    other = lax.ppermute(away, "y", near_y)
    low, high = jnp.where(odd, other, mine), jnp.where(odd, mine, other)

    conv = inverse(1.0, moved)
    back = inverse(-1.0, spec)
    returned = lax.all_to_all(
        jnp.concatenate([conv, back], axis=1), SEQ, split_axis=0, concat_axis=0, tiled=True
    )

    rows_out = [jnp.stack([low[n], high[n]]) for n in range(2)]
    rows_out = [jnp.where(upper_zhi, rows_out[1 - n], rows_out[n]) for n in range(2)]
    ends = [
        lax.ppermute(rows_out[number], everyone, [(b, a) for a, b in pairs[number]])
        for number in range(2)
    ]
    grad_filter = (
        (ends[0] + ends[1])
        .reshape(2, 2, per_seq, positions)
        .transpose(1, 0, 2, 3)
        .reshape(2, 2 * per_seq, positions)
    )

    scale = 1.0 / math.sqrt(seq_count * positions)
    conv = returned[:, : per_seq * positions].reshape(1, channels, positions) * scale
    backward = returned[:, per_seq * positions :].reshape(1, channels, positions) * scale
    grad_gate = (upstream * conv).astype(bf16)
    return (backward.astype(bf16), grad_gate, grad_filter)


def solution(mesh):
    split = Mesh(mesh.devices.reshape(2, 4, 2, 8, 4), DP + SEQ)
    return jax.shard_map(
        step,
        mesh=split,
        in_specs=(P(DP, None, SEQ), P(DP, None, SEQ), P(DP, None, None, SEQ), P(None, DP, SEQ)),
        out_specs=(P(DP, None, SEQ), P(DP, None, SEQ), P(None, DP, SEQ)),
        check_vma=False,
    )
```

```python
import functools
import math

import jax
import jax.numpy as jnp
import numpy as np
from jax import lax
from jax.experimental import pallas as pl
from jax.experimental.pallas import tpu as pltpu
from jax.sharding import Mesh, PartitionSpec as P


f32 = jnp.float32
bf16 = jnp.bfloat16
SEQ = ("zlo", "y")
DP = ("zhi", "x", "core")
MIB = 1024 * 1024


def unit_roots(rows, columns, period):
    product = np.outer(np.arange(rows, dtype=np.int64), np.arange(columns, dtype=np.int64))
    angle = (product % period).astype(np.float64) * (2.0 * np.pi / period)
    return np.cos(angle).astype(np.float32), np.sin(angle).astype(np.float32)


def halves(values):
    high = values.astype(bf16)
    return high, (values - high.astype(f32)).astype(bf16)


def three_terms(values, axis):
    high, low = halves(values)
    return jnp.concatenate([high, low, high], axis=axis)


def small_table(points, inverse):
    cosine, sine = unit_roots(points, points, points)
    whole = np.concatenate([cosine, -sine], axis=1 if inverse else 0)
    high = whole.astype(bf16)
    low = (whole - high.astype(np.float32)).astype(bf16)
    return jnp.asarray(np.concatenate([high, high, low], axis=1))


def dot16(left, right):
    return jnp.dot(left, right, preferred_element_type=f32)


def tables_kernel(coarse_ref, fine_ref, cos_hi, cos_lo, sin_hi, sin_lo):
    steps = fine_ref.shape[1]

    @pl.loop(0, coarse_ref.shape[1])
    def _(a):
        at = pl.ds(pl.multiple_of(a * steps, steps), steps)
        coarse_cos, coarse_sin = coarse_ref[0, pl.ds(a, 1), :], coarse_ref[1, pl.ds(a, 1), :]
        fine_cos, fine_sin = fine_ref[0], fine_ref[1]
        cosine = coarse_cos * fine_cos - coarse_sin * fine_sin
        sine = coarse_sin * fine_cos + coarse_cos * fine_sin
        cos_hi[at, :], cos_lo[at, :] = halves(cosine)
        sin_hi[at, :], sin_lo[at, :] = halves(sine)


def root_tables(points):
    steps, columns = 32, points // 4
    coarse = jnp.asarray(np.stack(unit_roots(points // steps, columns, points // steps)))
    fine = jnp.asarray(np.stack(unit_roots(steps, columns, points)))
    return pl.pallas_call(
        tables_kernel,
        out_shape=[jax.ShapeDtypeStruct((points, columns), bf16)] * 4,
        name="root_tables",
        compiler_params=pltpu.CompilerParams(vmem_limit_bytes=16 * MIB),
        cost_estimate=pl.CostEstimate(
            flops=20 * points * columns, bytes_accessed=8 * points * columns, transcendentals=0
        ),
    )(coarse, fine)


def keep_quarters(rows_ref, place, count, real, imag, conjugate):
    rows, points = real.shape
    lane = lax.broadcasted_iota(jnp.int32, (1, points), 1)
    odd = lane % 2 == 1
    alternate = jnp.where(odd, -1.0, 1.0)
    early = jnp.where(lane % 4 < 2, 1.0, -1.0)
    outer = jnp.where((lane + 1) % 4 < 2, 1.0, -1.0)
    swap_real, swap_imag = jnp.where(odd, imag, real), jnp.where(odd, real, imag)
    turned = [
        (real, imag),
        (swap_real * outer, swap_imag * early),
        (real * alternate, imag * alternate),
        (swap_real * early, swap_imag * outer),
    ]
    if conjugate:
        turned[1], turned[3] = turned[3], turned[1]
    for m in range(4):
        for part, values in enumerate(turned[m]):
            high, low = halves(values)
            first = (part * count + place) * rows
            rows_ref[m, first : first + rows, :] = high
            rows_ref[m, 2 * count * rows + first : 2 * count * rows + first + rows, :] = low


def root_product(high_low, hi_ref, lo_ref):
    rows = high_low.shape[0] // 2
    both = dot16(high_low, hi_ref[...])
    return both[:rows] + both[rows:] + dot16(high_low[:rows], lo_ref[...])


def forward_kernel(
    moved_ref, small_ref, twiddle_ref, cos_hi, cos_lo, sin_hi, sin_lo, spec_ref, terms_ref, rows_ref
):
    classes = moved_ref.shape[0]
    points = cos_hi.shape[0]
    scale = 1.0 / math.sqrt(classes * points)
    tw_cos, tw_sin = twiddle_ref[0] * scale, twiddle_ref[1] * scale
    for channel in range(2):
        delta = moved_ref[:, (4 + channel) * points : (5 + channel) * points]
        part = dot16(small_ref[...], three_terms(delta, 0))
        part_real, part_imag = part[:classes], part[classes:]
        turned_real = part_real * tw_cos + part_imag * tw_sin
        turned_imag = part_imag * tw_cos - part_real * tw_sin
        keep_quarters(rows_ref, channel, 2, turned_real, turned_imag, True)
    half = 2 * classes
    width = points // 4
    for tile in range(4):
        at = slice(tile * width, (tile + 1) * width)
        by_cos = root_product(rows_ref[tile], cos_hi, cos_lo)
        by_sin = root_product(rows_ref[tile], sin_hi, sin_lo)
        real = by_cos[:half] + by_sin[half:]
        imag = by_cos[half:] - by_sin[:half]
        for channel in range(2):
            mine = slice(channel * classes, (channel + 1) * classes)
            put_real = slice(channel * points + at.start, channel * points + at.stop)
            put_imag = slice((2 + channel) * points + at.start, (2 + channel) * points + at.stop)
            in_real, in_imag = moved_ref[:, put_real], moved_ref[:, put_imag]
            spec_ref[:, put_real] = real[mine]
            spec_ref[:, put_imag] = imag[mine]
            terms_ref[:, put_real] = in_real * real[mine] + in_imag * imag[mine]
            terms_ref[:, put_imag] = in_real * imag[mine] - in_imag * real[mine]


def inverse_kernel(
    sign, first_ref, filt_ref, small_ref, twiddle_ref, cos_hi, cos_lo, sin_hi, sin_lo, out_ref,
    rows_ref, turned_ref,
):
    classes = first_ref.shape[0]
    points = cos_hi.shape[0]

    for channel in range(2):
        real_at = slice(channel * points, (channel + 1) * points)
        imag_at = slice((2 + channel) * points, (3 + channel) * points)
        filt_real, filt_imag = filt_ref[:, real_at], filt_ref[:, imag_at] * sign
        first_real, first_imag = first_ref[:, real_at], first_ref[:, imag_at]
        keep_quarters(
            rows_ref,
            channel,
            2,
            first_real * filt_real - first_imag * filt_imag,
            first_real * filt_imag + first_imag * filt_real,
            False,
        )
    half = 2 * classes
    width = points // 4
    for tile in range(4):
        at = slice(tile * width, (tile + 1) * width)
        by_cos = root_product(rows_ref[tile], cos_hi, cos_lo)
        by_sin = root_product(rows_ref[tile], sin_hi, sin_lo)
        real = by_cos[:half] - by_sin[half:]
        imag = by_cos[half:] + by_sin[:half]
        tw_cos, tw_sin = twiddle_ref[0, :, at], twiddle_ref[1, :, at]
        for channel in range(2):
            mine = slice(channel * classes, (channel + 1) * classes)
            put = slice(channel * points + at.start, channel * points + at.stop)
            for part, turned in (
                (0, real[mine] * tw_cos - imag[mine] * tw_sin),
                (1, imag[mine] * tw_cos + real[mine] * tw_sin),
            ):
                high, low = halves(turned)
                for place, values in ((part, high), (2 + part, low), (4 + part, high)):
                    turned_ref[place * classes : (place + 1) * classes, put] = values
    out_ref[...] = dot16(small_ref[...], turned_ref[...])


def staging_pairs(x_count, core_count, seq_count):
    pairs = []
    for number in range(2):
        found = []
        for d in range(2 * x_count * core_count):
            for s in range(seq_count):
                e0, core, near, far, e1 = [s >> bit & 1 for bit in (4, 3, 2, 1, 0)]
                row = ((e1 ^ number) * x_count + 2 * far + near) * core_count + core
                found.append((d * seq_count + s, row * seq_count + 2 * d + e0))
        pairs.append(found)
    return pairs


def halving(values, upper, axis, pairs):
    rows = values.shape[0] // 2
    kept = jnp.where(upper, values[rows:], values[:rows])
    away = jnp.where(upper, values[:rows], values[rows:])
    return kept + lax.ppermute(away, axis, pairs)


def doubling(values, upper, axis, pairs):
    other = lax.ppermute(values, axis, pairs)
    return jnp.concatenate(
        [jnp.where(upper, other, values), jnp.where(upper, values, other)], axis=0
    )


def step(grad_out, gate, input_spectrum, filter_spectrum):
    _, channels, positions = grad_out.shape
    seq_count = lax.axis_size(SEQ)
    x_count = lax.axis_size("x")
    everyone = DP + SEQ
    odd = lax.axis_index(SEQ) % 2 == 1
    upper_zhi = lax.axis_index("zhi") == 1
    upper_core = lax.axis_index("core") == 1
    x_index = lax.axis_index("x")
    pairs = staging_pairs(x_count, 2, seq_count)
    per_seq = channels // seq_count

    upstream = grad_out.astype(f32)
    delta = (upstream * gate.astype(f32)).reshape(seq_count, per_seq * positions)
    spectrum = (
        input_spectrum.reshape(2, seq_count, per_seq, positions)
        .transpose(1, 0, 2, 3)
        .reshape(seq_count, 2 * per_seq * positions)
    )
    moved = lax.all_to_all(
        jnp.concatenate([spectrum, delta], axis=1), SEQ, split_axis=0, concat_axis=0, tiled=True
    )

    near_x = [(x, x ^ 1) for x in range(x_count)]
    far_x = [(x, x ^ 2) for x in range(x_count)]
    near_y = [(y, y ^ 1) for y in range(lax.axis_size("y"))]
    cores = [(0, 1), (1, 0)]
    half_row = 4 * positions
    sent = (
        filter_spectrum.reshape(2, 2, per_seq, positions)
        .transpose(1, 0, 2, 3)
        .reshape(1, 2 * half_row)
    )
    got = [lax.ppermute(sent, everyone, pairs[number]) for number in range(2)]
    filters = jnp.concatenate(
        [jnp.where(upper_zhi, got[1], got[0]), jnp.where(upper_zhi, got[0], got[1])], axis=0
    )
    filters = doubling(filters, x_index >= 2, "x", far_x)
    filters = doubling(filters, x_index % 2 == 1, "x", near_x)
    filters = doubling(filters, upper_core, "core", cores)
    mine = jnp.where(odd, filters[:, half_row:], filters[:, :half_row])
    away = jnp.where(odd, filters[:, :half_row], filters[:, half_row:])
    other = lax.ppermute(away, "y", near_y)
    filters = jnp.concatenate([jnp.where(odd, other, mine), jnp.where(odd, mine, other)], axis=0)

    tables = root_tables(positions)
    small_out = small_table(seq_count, False)
    small_back = small_table(seq_count, True)
    twiddle = jnp.asarray(np.stack(unit_roots(seq_count, positions, seq_count * positions)))

    wide = jax.ShapeDtypeStruct((seq_count, 4 * positions), f32)
    signal = jax.ShapeDtypeStruct((seq_count, 2 * positions), f32)
    rows = [pltpu.VMEM((4, 8 * seq_count, positions), bf16)]
    params = pltpu.CompilerParams(vmem_limit_bytes=16 * MIB)
    cost = pl.CostEstimate(flops=2 * 10**9, bytes_accessed=10**7, transcendentals=0)
    spec, terms = pl.pallas_call(
        forward_kernel,
        out_shape=[wide, wide],
        scratch_shapes=rows,
        name="forward",
        compiler_params=params,
        cost_estimate=cost,
    )(moved, small_out, twiddle, *tables)

    def inverse(sign, first):
        return pl.pallas_call(
            functools.partial(inverse_kernel, sign),
            out_shape=signal,
            scratch_shapes=rows + [pltpu.VMEM((6 * seq_count, 2 * positions), bf16)],
            name="inverse",
            compiler_params=params,
            cost_estimate=cost,
        )(first, filters, small_back, twiddle, *tables)

    half = seq_count // 2
    mine = jnp.where(odd, terms[half:], terms[:half])
    away = jnp.where(odd, terms[:half], terms[half:])
    other = lax.ppermute(away, "y", near_y)
    total = jnp.concatenate(
        [jnp.where(odd, other, mine), jnp.where(odd, mine, other)], axis=1
    )
    total = halving(total, upper_core, "core", cores)
    total = halving(total, x_index % 2 == 1, "x", near_x)
    total = halving(total, x_index >= 2, "x", far_x)

    conv = inverse(1.0, moved)
    back = inverse(-1.0, spec)
    returned = lax.all_to_all(
        jnp.concatenate([conv, back], axis=1), SEQ, split_axis=0, concat_axis=0, tiled=True
    )

    rows_out = [
        jnp.where(upper_zhi, total[1 - n : 2 - n], total[n : n + 1]) for n in range(2)
    ]
    ends = [
        lax.ppermute(rows_out[number], everyone, [(b, a) for a, b in pairs[number]])
        for number in range(2)
    ]
    grad_filter = (
        (ends[0] + ends[1])
        .reshape(2, 2, per_seq, positions)
        .transpose(1, 0, 2, 3)
        .reshape(2, 2 * per_seq, positions)
    )

    scale = 1.0 / math.sqrt(seq_count * positions)
    conv = returned[:, : per_seq * positions].reshape(1, channels, positions) * scale
    backward = returned[:, per_seq * positions :].reshape(1, channels, positions) * scale
    grad_gate = (upstream * conv).astype(bf16)
    return (backward.astype(bf16), grad_gate, grad_filter)


def solution(mesh):
    split = Mesh(mesh.devices.reshape(2, 4, 2, 8, 4), DP + SEQ)
    return jax.shard_map(
        step,
        mesh=split,
        in_specs=(P(DP, None, SEQ), P(DP, None, SEQ), P(DP, None, None, SEQ), P(None, DP, SEQ)),
        out_specs=(P(DP, None, SEQ), P(DP, None, SEQ), P(None, DP, SEQ)),
        check_vma=False,
    )
```

```python
import math

import jax
import jax.numpy as jnp
import numpy as np
from jax import lax
from jax.experimental import pallas as pl
from jax.experimental.pallas import tpu as pltpu
from jax.sharding import Mesh, PartitionSpec as P


f32 = jnp.float32
bf16 = jnp.bfloat16
SEQ = ("zlo", "y")
DP = ("zhi", "x", "core")
MIB = 1024 * 1024


def unit_roots(rows, columns, period):
    product = np.outer(np.arange(rows, dtype=np.int64), np.arange(columns, dtype=np.int64))
    angle = (product % period).astype(np.float64) * (2.0 * np.pi / period)
    return np.cos(angle).astype(np.float32), np.sin(angle).astype(np.float32)


def halves(values):
    high = values.astype(bf16)
    return high, (values - high.astype(f32)).astype(bf16)


def three_terms(values, axis):
    high, low = halves(values)
    return jnp.concatenate([high, low, high], axis=axis)


def small_table(points, inverse):
    cosine, sine = unit_roots(points, points, points)
    whole = np.concatenate([cosine, -sine], axis=1 if inverse else 0)
    high = whole.astype(bf16)
    low = (whole - high.astype(np.float32)).astype(bf16)
    return jnp.asarray(np.concatenate([high, high, low], axis=1))


def dot16(left, right):
    return jnp.dot(left, right, preferred_element_type=f32)


def tables_kernel(coarse_ref, fine_ref, cos_hi, cos_lo, sin_hi, sin_lo):
    steps = fine_ref.shape[1]

    @pl.loop(0, coarse_ref.shape[1])
    def _(a):
        at = pl.ds(pl.multiple_of(a * steps, steps), steps)
        coarse_cos, coarse_sin = coarse_ref[0, pl.ds(a, 1), :], coarse_ref[1, pl.ds(a, 1), :]
        fine_cos, fine_sin = fine_ref[0], fine_ref[1]
        cosine = coarse_cos * fine_cos - coarse_sin * fine_sin
        sine = coarse_sin * fine_cos + coarse_cos * fine_sin
        cos_hi[at, :], cos_lo[at, :] = halves(cosine)
        sin_hi[at, :], sin_lo[at, :] = halves(sine)


def root_tables(points):
    steps, columns = 32, points // 4
    coarse = jnp.asarray(np.stack(unit_roots(points // steps, columns, points // steps)))
    fine = jnp.asarray(np.stack(unit_roots(steps, columns, points)))
    return pl.pallas_call(
        tables_kernel,
        out_shape=[jax.ShapeDtypeStruct((points, columns), bf16)] * 4,
        name="root_tables",
        compiler_params=pltpu.CompilerParams(vmem_limit_bytes=16 * MIB),
        cost_estimate=pl.CostEstimate(
            flops=20 * points * columns, bytes_accessed=8 * points * columns, transcendentals=0
        ),
    )(coarse, fine)


def keep_quarters(rows_ref, place, count, real, imag, conjugate):
    rows, points = real.shape
    lane = lax.broadcasted_iota(jnp.int32, (1, points), 1)
    odd = lane % 2 == 1
    alternate = jnp.where(odd, -1.0, 1.0)
    early = jnp.where(lane % 4 < 2, 1.0, -1.0)
    outer = jnp.where((lane + 1) % 4 < 2, 1.0, -1.0)
    swap_real, swap_imag = jnp.where(odd, imag, real), jnp.where(odd, real, imag)
    turned = [
        (real, imag),
        (swap_real * outer, swap_imag * early),
        (real * alternate, imag * alternate),
        (swap_real * early, swap_imag * outer),
    ]
    if conjugate:
        turned[1], turned[3] = turned[3], turned[1]
    for m in range(4):
        for part, values in enumerate(turned[m]):
            high, low = halves(values)
            first = (part * count + place) * rows
            rows_ref[m, first : first + rows, :] = high
            rows_ref[m, 2 * count * rows + first : 2 * count * rows + first + rows, :] = low


def root_product(high_low, hi_ref, lo_ref):
    rows = high_low.shape[0] // 2
    both = dot16(high_low, hi_ref[...])
    return both[:rows] + both[rows:] + dot16(high_low[:rows], lo_ref[...])


def pack_kernel(out_ref, gate_ref, spec_ref, packed_ref, rows_ref):
    points = out_ref.shape[2]
    count = packed_ref.shape[0]
    for source in range(3):
        for start in range(0, points, 128):
            cut = slice(start, start + 128)
            slot = source * (points // 128) + start // 128
            if source == 2:
                rows_ref[slot] = out_ref[0, :, cut].astype(f32) * gate_ref[0, :, cut].astype(f32)
            else:
                rows_ref[slot] = spec_ref[0, source, :, cut]
            for channel in range(2):
                at = (2 * source + channel) * points + start
                packed_ref[:, 0, at : at + 128] = rows_ref[slot, pl.ds(channel, count, stride=2), :]


def forward_kernel(
    odd_ref, moved_ref, small_ref, twiddle_ref, cos_hi, cos_lo, sin_hi, sin_lo, spec_ref, mine_ref,
    away_ref, rows_ref,
):
    classes = moved_ref.shape[0]
    points = cos_hi.shape[0]
    scale = 1.0 / math.sqrt(classes * points)
    odd = odd_ref[0] == 1
    tw_cos, tw_sin = twiddle_ref[0] * scale, twiddle_ref[1] * scale
    for channel in range(2):
        delta = moved_ref[:, (4 + channel) * points : (5 + channel) * points]
        part = dot16(small_ref[...], three_terms(delta, 0))
        part_real, part_imag = part[:classes], part[classes:]
        turned_real = part_real * tw_cos + part_imag * tw_sin
        turned_imag = part_imag * tw_cos - part_real * tw_sin
        keep_quarters(rows_ref, channel, 2, turned_real, turned_imag, True)
    half = 2 * classes
    width = points // 4
    for tile in range(4):
        at = slice(tile * width, (tile + 1) * width)
        by_cos = root_product(rows_ref[tile], cos_hi, cos_lo)
        by_sin = root_product(rows_ref[tile], sin_hi, sin_lo)
        real = by_cos[:half] + by_sin[half:]
        imag = by_cos[half:] - by_sin[:half]
        for channel in range(2):
            mine = slice(channel * classes, (channel + 1) * classes)
            put_real = slice(channel * points + at.start, channel * points + at.stop)
            put_imag = slice((2 + channel) * points + at.start, (2 + channel) * points + at.stop)
            in_real, in_imag = moved_ref[:, put_real], moved_ref[:, put_imag]
            spec_ref[:, put_real] = real[mine]
            spec_ref[:, put_imag] = imag[mine]
            term_real = in_real * real[mine] + in_imag * imag[mine]
            term_imag = in_real * imag[mine] - in_imag * real[mine]
            for put, term in ((put_real, term_real), (put_imag, term_imag)):
                lower, upper = term[: classes // 2], term[classes // 2 :]
                mine_ref[:, put] = jnp.where(odd, upper, lower)
                away_ref[:, put] = jnp.where(odd, lower, upper)


def inverse_rows(
    sign, odd_ref, first_ref, mine_ref, other_ref, small_ref, twiddle_ref, tables, rows_ref,
    turned_ref,
):
    cos_hi, cos_lo, sin_hi, sin_lo = tables
    classes = first_ref.shape[0]
    points = cos_hi.shape[0]
    odd = odd_ref[0] == 1

    def filt(at):
        mine, other = mine_ref[:, at], other_ref[:, at]
        return jnp.concatenate([jnp.where(odd, other, mine), jnp.where(odd, mine, other)], axis=0)

    for channel in range(2):
        real_at = slice(channel * points, (channel + 1) * points)
        imag_at = slice((2 + channel) * points, (3 + channel) * points)
        filt_real, filt_imag = filt(real_at), filt(imag_at) * sign
        first_real, first_imag = first_ref[:, real_at], first_ref[:, imag_at]
        keep_quarters(
            rows_ref,
            channel,
            2,
            first_real * filt_real - first_imag * filt_imag,
            first_real * filt_imag + first_imag * filt_real,
            False,
        )
    half = 2 * classes
    width = points // 4
    for tile in range(4):
        at = slice(tile * width, (tile + 1) * width)
        by_cos = root_product(rows_ref[tile], cos_hi, cos_lo)
        by_sin = root_product(rows_ref[tile], sin_hi, sin_lo)
        real = by_cos[:half] - by_sin[half:]
        imag = by_cos[half:] + by_sin[:half]
        tw_cos, tw_sin = twiddle_ref[0, :, at], twiddle_ref[1, :, at]
        for channel in range(2):
            mine = slice(channel * classes, (channel + 1) * classes)
            put = slice(channel * points + at.start, channel * points + at.stop)
            for part, turned in (
                (0, real[mine] * tw_cos - imag[mine] * tw_sin),
                (1, imag[mine] * tw_cos + real[mine] * tw_sin),
            ):
                high, low = halves(turned)
                for place, values in ((part, high), (2 + part, low), (4 + part, high)):
                    turned_ref[place * classes : (place + 1) * classes, put] = values
    return dot16(small_ref[...], turned_ref[...])


def conv_kernel(
    odd_ref, moved_ref, mine_ref, other_ref, small_ref, twiddle_ref, cos_hi, cos_lo, sin_hi, sin_lo,
    conv_ref, rows_ref, turned_ref,
):
    tables = (cos_hi, cos_lo, sin_hi, sin_lo)
    conv_ref[...] = inverse_rows(
        1.0, odd_ref, moved_ref, mine_ref, other_ref, small_ref, twiddle_ref, tables, rows_ref,
        turned_ref,
    )


def back_kernel(
    odd_ref, conv_ref, spec_ref, mine_ref, other_ref, small_ref, twiddle_ref, cos_hi, cos_lo,
    sin_hi, sin_lo, packed_ref, rows_ref, turned_ref,
):
    tables = (cos_hi, cos_lo, sin_hi, sin_lo)
    width = conv_ref.shape[1]
    packed_ref[:, 0, :width] = conv_ref[...]
    packed_ref[:, 0, width:] = inverse_rows(
        -1.0, odd_ref, spec_ref, mine_ref, other_ref, small_ref, twiddle_ref, tables, rows_ref,
        turned_ref,
    )


def staging_pairs(x_count, core_count, seq_count):
    pairs = []
    for number in range(2):
        found = []
        for d in range(2 * x_count * core_count):
            for s in range(seq_count):
                e0, core, near, far, e1 = [s >> bit & 1 for bit in (4, 3, 2, 1, 0)]
                row = ((e1 ^ number) * x_count + 2 * far + near) * core_count + core
                found.append((d * seq_count + s, row * seq_count + 2 * d + e0))
        pairs.append(found)
    return pairs


def kept_and_away(values, upper):
    half = values.shape[1] // 2
    lower, higher = values[:, :half], values[:, half:]
    return jnp.where(upper, higher, lower), jnp.where(upper, lower, higher)


def halving(values, upper, axis, pairs):
    kept, away = kept_and_away(values, upper)
    return kept + lax.ppermute(away, axis, pairs)


def doubling(values, upper, axis, pairs):
    other = lax.ppermute(values, axis, pairs)
    return jnp.concatenate(
        [jnp.where(upper, other, values), jnp.where(upper, values, other)], axis=0
    )


def step(grad_out, gate, input_spectrum, filter_spectrum):
    _, channels, positions = grad_out.shape
    seq_count = lax.axis_size(SEQ)
    x_count = lax.axis_size("x")
    everyone = DP + SEQ
    odd = lax.axis_index(SEQ) % 2 == 1
    upper_zhi = lax.axis_index("zhi") == 1
    upper_core = lax.axis_index("core") == 1
    x_index = lax.axis_index("x")
    pairs = staging_pairs(x_count, 2, seq_count)
    per_seq = channels // seq_count

    params = pltpu.CompilerParams(vmem_limit_bytes=16 * MIB)
    packed = pl.pallas_call(
        pack_kernel,
        out_shape=jax.ShapeDtypeStruct((seq_count, 1, 3 * per_seq * positions), f32),
        scratch_shapes=[pltpu.VMEM((3 * positions // 128, channels, 128), f32)],
        name="pack",
        compiler_params=params,
        cost_estimate=pl.CostEstimate(flops=10**5, bytes_accessed=2 * 10**6, transcendentals=0),
    )(grad_out, gate, input_spectrum)
    moved = lax.all_to_all(packed, SEQ, split_axis=0, concat_axis=0, tiled=True)
    moved = moved.reshape(seq_count, 3 * per_seq * positions)

    near_x = [(x, x ^ 1) for x in range(x_count)]
    far_x = [(x, x ^ 2) for x in range(x_count)]
    near_y = [(y, y ^ 1) for y in range(lax.axis_size("y"))]
    cores = [(0, 1), (1, 0)]
    half_row = 4 * positions
    sent = (
        filter_spectrum.reshape(2, 2, per_seq, positions)
        .transpose(1, 0, 2, 3)
        .reshape(1, 2 * half_row)
    )
    got = [lax.ppermute(sent, everyone, pairs[number]) for number in range(2)]
    filters = jnp.concatenate(
        [jnp.where(upper_zhi, got[1], got[0]), jnp.where(upper_zhi, got[0], got[1])], axis=0
    )
    filters = doubling(filters, x_index >= 2, "x", far_x)
    filters = doubling(filters, x_index % 2 == 1, "x", near_x)
    filters = doubling(filters, upper_core, "core", cores)
    mine = jnp.where(odd, filters[:, half_row:], filters[:, :half_row])
    away = jnp.where(odd, filters[:, :half_row], filters[:, half_row:])
    filters = (mine, lax.ppermute(away, "y", near_y))

    tables = root_tables(positions)
    small_out = small_table(seq_count, False)
    small_back = small_table(seq_count, True)
    twiddle = jnp.asarray(np.stack(unit_roots(seq_count, positions, seq_count * positions)))

    half = seq_count // 2
    parity = odd.astype(jnp.int32).reshape(1)
    wide = jax.ShapeDtypeStruct((seq_count, half_row), f32)
    narrow = jax.ShapeDtypeStruct((half, half_row), f32)
    rows = [pltpu.VMEM((4, 8 * seq_count, positions), bf16)]
    turned = [pltpu.VMEM((6 * seq_count, 2 * positions), bf16)]
    cost = pl.CostEstimate(flops=2 * 10**9, bytes_accessed=10**7, transcendentals=0)

    def specs(count):
        return [pl.BlockSpec(memory_space=pltpu.SMEM)] + [
            pl.BlockSpec(memory_space=pltpu.VMEM) for _ in range(count)
        ]

    spec, mine, away = pl.pallas_call(
        forward_kernel,
        out_shape=[wide, narrow, narrow],
        in_specs=specs(7),
        scratch_shapes=rows,
        name="forward",
        compiler_params=params,
        cost_estimate=cost,
    )(parity, moved, small_out, twiddle, *tables)

    other = lax.ppermute(away, "y", near_y)
    total = halving(jnp.stack([mine, other]), upper_core, "core", cores)
    total = halving(total, x_index % 2 == 1, "x", near_x)
    total = halving(total, x_index >= 2, "x", far_x)

    conv = pl.pallas_call(
        conv_kernel,
        out_shape=jax.ShapeDtypeStruct((seq_count, 2 * positions), f32),
        in_specs=specs(9),
        scratch_shapes=rows + turned,
        name="conv",
        compiler_params=params,
        cost_estimate=cost,
    )(parity, moved, *filters, small_back, twiddle, *tables)
    signals = pl.pallas_call(
        back_kernel,
        out_shape=jax.ShapeDtypeStruct((seq_count, 1, 4 * positions), f32),
        in_specs=specs(10),
        scratch_shapes=rows + turned,
        name="back",
        compiler_params=params,
        cost_estimate=cost,
    )(parity, conv, spec, *filters, small_back, twiddle, *tables)
    returned = lax.all_to_all(signals, SEQ, split_axis=0, concat_axis=0, tiled=True)
    returned = returned.reshape(seq_count, 4 * positions)

    ordered = jnp.where(odd, total[::-1], total)
    rows_out = [jnp.where(upper_zhi, ordered[:, 1 - n], ordered[:, n]) for n in range(2)]
    ends = [
        lax.ppermute(rows_out[number], everyone, [(b, a) for a, b in pairs[number]])
        for number in range(2)
    ]
    grad_filter = (
        (ends[0] + ends[1])
        .reshape(2, 2, per_seq, positions)
        .transpose(1, 0, 2, 3)
        .reshape(2, 2 * per_seq, positions)
    )

    scale = 1.0 / math.sqrt(seq_count * positions)
    conv = returned[:, : per_seq * positions].reshape(1, channels, positions) * scale
    backward = returned[:, per_seq * positions :].reshape(1, channels, positions) * scale
    grad_gate = (grad_out.astype(f32) * conv).astype(bf16)
    return (backward.astype(bf16), grad_gate, grad_filter)


def solution(mesh):
    split = Mesh(mesh.devices.reshape(2, 4, 2, 8, 4), DP + SEQ)
    return jax.shard_map(
        step,
        mesh=split,
        in_specs=(P(DP, None, SEQ), P(DP, None, SEQ), P(DP, None, None, SEQ), P(None, DP, SEQ)),
        out_specs=(P(DP, None, SEQ), P(DP, None, SEQ), P(None, DP, SEQ)),
        check_vma=False,
    )
```

```python
import math

import jax
import jax.numpy as jnp
import numpy as np
from jax import lax
from jax.experimental import pallas as pl
from jax.experimental.pallas import tpu as pltpu
from jax.sharding import Mesh, PartitionSpec as P


f32 = jnp.float32
bf16 = jnp.bfloat16
SEQ = ("zlo", "y")
DP = ("zhi", "x", "core")
MIB = 1024 * 1024


def unit_roots(rows, columns, period):
    product = np.outer(np.arange(rows, dtype=np.int64), np.arange(columns, dtype=np.int64))
    angle = (product % period).astype(np.float64) * (2.0 * np.pi / period)
    return np.cos(angle).astype(np.float32), np.sin(angle).astype(np.float32)


def halves(values):
    high = values.astype(bf16)
    return high, (values - high.astype(f32)).astype(bf16)


def three_terms(values, axis):
    high, low = halves(values)
    return jnp.concatenate([high, low, high], axis=axis)


def small_table(points, inverse):
    cosine, sine = unit_roots(points, points, points)
    whole = np.concatenate([cosine, -sine], axis=1 if inverse else 0)
    high = whole.astype(bf16)
    low = (whole - high.astype(np.float32)).astype(bf16)
    return jnp.asarray(np.concatenate([high, high, low], axis=1))


def dot16(left, right):
    return jnp.dot(left, right, preferred_element_type=f32)


def tables_kernel(coarse_ref, fine_ref, cos_hi, cos_lo, sin_hi, sin_lo):
    steps = fine_ref.shape[1]

    @pl.loop(0, coarse_ref.shape[1])
    def _(a):
        at = pl.ds(pl.multiple_of(a * steps, steps), steps)
        coarse_cos, coarse_sin = coarse_ref[0, pl.ds(a, 1), :], coarse_ref[1, pl.ds(a, 1), :]
        fine_cos, fine_sin = fine_ref[0], fine_ref[1]
        cosine = coarse_cos * fine_cos - coarse_sin * fine_sin
        sine = coarse_sin * fine_cos + coarse_cos * fine_sin
        cos_hi[at, :], cos_lo[at, :] = halves(cosine)
        sin_hi[at, :], sin_lo[at, :] = halves(sine)


def root_tables(points):
    steps, columns = 32, points // 4
    coarse = jnp.asarray(np.stack(unit_roots(points // steps, columns, points // steps)))
    fine = jnp.asarray(np.stack(unit_roots(steps, columns, points)))
    return pl.pallas_call(
        tables_kernel,
        out_shape=[jax.ShapeDtypeStruct((points, columns), bf16)] * 4,
        name="root_tables",
        compiler_params=pltpu.CompilerParams(vmem_limit_bytes=16 * MIB),
        cost_estimate=pl.CostEstimate(
            flops=20 * points * columns, bytes_accessed=8 * points * columns, transcendentals=0
        ),
    )(coarse, fine)


def keep_quarters(rows_ref, place, count, real, imag, conjugate):
    rows, points = real.shape
    lane = lax.broadcasted_iota(jnp.int32, (1, points), 1)
    odd = lane % 2 == 1
    alternate = jnp.where(odd, -1.0, 1.0)
    early = jnp.where(lane % 4 < 2, 1.0, -1.0)
    outer = jnp.where((lane + 1) % 4 < 2, 1.0, -1.0)
    swap_real, swap_imag = jnp.where(odd, imag, real), jnp.where(odd, real, imag)
    turned = [
        (real, imag),
        (swap_real * outer, swap_imag * early),
        (real * alternate, imag * alternate),
        (swap_real * early, swap_imag * outer),
    ]
    if conjugate:
        turned[1], turned[3] = turned[3], turned[1]
    for m in range(4):
        for part, values in enumerate(turned[m]):
            high, low = halves(values)
            first = (part * count + place) * rows
            rows_ref[m, first : first + rows, :] = high
            rows_ref[m, 2 * count * rows + first : 2 * count * rows + first + rows, :] = low


def root_product(high_low, hi_ref, lo_ref):
    rows = high_low.shape[0] // 2
    both = dot16(high_low, hi_ref[...])
    return both[:rows] + both[rows:] + dot16(high_low[:rows], lo_ref[...])


def pack_kernel(out_ref, gate_ref, spec_ref, packed_ref, rows_ref):
    points = out_ref.shape[2]
    count = packed_ref.shape[0]
    for source in range(3):
        for start in range(0, points, 128):
            cut = slice(start, start + 128)
            slot = source * (points // 128) + start // 128
            if source == 2:
                rows_ref[slot] = out_ref[0, :, cut].astype(f32) * gate_ref[0, :, cut].astype(f32)
            else:
                rows_ref[slot] = spec_ref[0, source, :, cut]
            for channel in range(2):
                at = (2 * source + channel) * points + start
                packed_ref[:, 0, at : at + 128] = rows_ref[slot, pl.ds(channel, count, stride=2), :]


def forward_kernel(
    core_ref, moved_ref, small_ref, twiddle_ref, cos_hi, cos_lo, sin_hi, sin_lo, spec_ref, kept_ref,
    away_ref, rows_ref,
):
    classes = moved_ref.shape[0]
    points = cos_hi.shape[0]
    scale = 1.0 / math.sqrt(classes * points)
    upper_core = core_ref[0] == 1
    quarter = classes // 4
    tw_cos, tw_sin = twiddle_ref[0] * scale, twiddle_ref[1] * scale
    for channel in range(2):
        delta = moved_ref[:, (4 + channel) * points : (5 + channel) * points]
        part = dot16(small_ref[...], three_terms(delta, 0))
        part_real, part_imag = part[:classes], part[classes:]
        turned_real = part_real * tw_cos + part_imag * tw_sin
        turned_imag = part_imag * tw_cos - part_real * tw_sin
        keep_quarters(rows_ref, channel, 2, turned_real, turned_imag, True)
    half = 2 * classes
    width = points // 4
    for tile in range(4):
        at = slice(tile * width, (tile + 1) * width)
        by_cos = root_product(rows_ref[tile], cos_hi, cos_lo)
        by_sin = root_product(rows_ref[tile], sin_hi, sin_lo)
        real = by_cos[:half] + by_sin[half:]
        imag = by_cos[half:] - by_sin[:half]
        for channel in range(2):
            mine = slice(channel * classes, (channel + 1) * classes)
            put_real = slice(channel * points + at.start, channel * points + at.stop)
            put_imag = slice((2 + channel) * points + at.start, (2 + channel) * points + at.stop)
            in_real, in_imag = moved_ref[:, put_real], moved_ref[:, put_imag]
            spec_ref[:, put_real] = real[mine]
            spec_ref[:, put_imag] = imag[mine]
            term_real = in_real * real[mine] + in_imag * imag[mine]
            term_imag = in_real * imag[mine] - in_imag * real[mine]
            for put, term in ((put_real, term_real), (put_imag, term_imag)):
                for side in range(2):
                    lower = term[2 * side * quarter : (2 * side + 1) * quarter]
                    upper = term[(2 * side + 1) * quarter : (2 * side + 2) * quarter]
                    kept_ref[side, :, put] = jnp.where(upper_core, upper, lower)
                    away_ref[side, :, put] = jnp.where(upper_core, lower, upper)


def inverse_rows(
    sign, first_ref, filt_ref, small_ref, twiddle_ref, tables, rows_ref, turned_ref
):
    cos_hi, cos_lo, sin_hi, sin_lo = tables
    classes = first_ref.shape[0]
    points = cos_hi.shape[0]
    for channel in range(2):
        real_at = slice(channel * points, (channel + 1) * points)
        imag_at = slice((2 + channel) * points, (3 + channel) * points)
        filt_real, filt_imag = filt_ref[:, real_at], filt_ref[:, imag_at] * sign
        first_real, first_imag = first_ref[:, real_at], first_ref[:, imag_at]
        keep_quarters(
            rows_ref,
            channel,
            2,
            first_real * filt_real - first_imag * filt_imag,
            first_real * filt_imag + first_imag * filt_real,
            False,
        )
    half = 2 * classes
    width = points // 4
    for tile in range(4):
        at = slice(tile * width, (tile + 1) * width)
        by_cos = root_product(rows_ref[tile], cos_hi, cos_lo)
        by_sin = root_product(rows_ref[tile], sin_hi, sin_lo)
        real = by_cos[:half] - by_sin[half:]
        imag = by_cos[half:] + by_sin[:half]
        tw_cos, tw_sin = twiddle_ref[0, :, at], twiddle_ref[1, :, at]
        for channel in range(2):
            mine = slice(channel * classes, (channel + 1) * classes)
            put = slice(channel * points + at.start, channel * points + at.stop)
            for part, turned in (
                (0, real[mine] * tw_cos - imag[mine] * tw_sin),
                (1, imag[mine] * tw_cos + real[mine] * tw_sin),
            ):
                high, low = halves(turned)
                for place, values in ((part, high), (2 + part, low), (4 + part, high)):
                    turned_ref[place * classes : (place + 1) * classes, put] = values
    return dot16(small_ref[...], turned_ref[...])


def conv_kernel(
    moved_ref, filt_ref, small_ref, twiddle_ref, cos_hi, cos_lo, sin_hi, sin_lo, conv_ref, rows_ref,
    turned_ref,
):
    tables = (cos_hi, cos_lo, sin_hi, sin_lo)
    conv_ref[...] = inverse_rows(
        1.0, moved_ref, filt_ref, small_ref, twiddle_ref, tables, rows_ref, turned_ref
    )


def back_kernel(
    conv_ref, spec_ref, filt_ref, small_ref, twiddle_ref, cos_hi, cos_lo, sin_hi, sin_lo, packed_ref,
    rows_ref, turned_ref,
):
    tables = (cos_hi, cos_lo, sin_hi, sin_lo)
    width = conv_ref.shape[1]
    packed_ref[:, 0, :width] = conv_ref[...]
    packed_ref[:, 0, width:] = inverse_rows(
        -1.0, spec_ref, filt_ref, small_ref, twiddle_ref, tables, rows_ref, turned_ref
    )


def staging_pairs(x_count, core_count, seq_count):
    pairs = []
    for number in range(2):
        found = []
        for d in range(2 * x_count * core_count):
            for s in range(seq_count):
                e0, core, near, far, e1 = [s >> bit & 1 for bit in (4, 3, 2, 1, 0)]
                row = ((e1 ^ number) * x_count + 2 * far + near) * core_count + core
                found.append((d * seq_count + s, row * seq_count + 2 * d + e0))
        pairs.append(found)
    return pairs


def kept_and_away(values, upper):
    half = values.shape[1] // 2
    lower, higher = values[:, :half], values[:, half:]
    return jnp.where(upper, higher, lower), jnp.where(upper, lower, higher)


def halving(values, upper, axis, pairs):
    kept, away = kept_and_away(values, upper)
    return kept + lax.ppermute(away, axis, pairs)


def doubling(values, upper, axis, pairs):
    other = lax.ppermute(values, axis, pairs)
    return jnp.concatenate(
        [jnp.where(upper, other, values), jnp.where(upper, values, other)], axis=1
    )


def step(grad_out, gate, input_spectrum, filter_spectrum):
    _, channels, positions = grad_out.shape
    seq_count = lax.axis_size(SEQ)
    x_count = lax.axis_size("x")
    everyone = DP + SEQ
    odd = lax.axis_index(SEQ) % 2 == 1
    upper_zhi = lax.axis_index("zhi") == 1
    upper_core = lax.axis_index("core") == 1
    x_index = lax.axis_index("x")
    pairs = staging_pairs(x_count, 2, seq_count)
    per_seq = channels // seq_count

    params = pltpu.CompilerParams(vmem_limit_bytes=16 * MIB)
    packed = pl.pallas_call(
        pack_kernel,
        out_shape=jax.ShapeDtypeStruct((seq_count, 1, 3 * per_seq * positions), f32),
        scratch_shapes=[pltpu.VMEM((3 * positions // 128, channels, 128), f32)],
        name="pack",
        compiler_params=params,
        cost_estimate=pl.CostEstimate(flops=10**5, bytes_accessed=2 * 10**6, transcendentals=0),
    )(grad_out, gate, input_spectrum)
    moved = lax.all_to_all(packed, SEQ, split_axis=0, concat_axis=0, tiled=True)
    moved = moved.reshape(seq_count, 3 * per_seq * positions)

    near_x = [(x, x ^ 1) for x in range(x_count)]
    far_x = [(x, x ^ 2) for x in range(x_count)]
    near_y = [(y, y ^ 1) for y in range(lax.axis_size("y"))]
    cores = [(0, 1), (1, 0)]
    half_row = 4 * positions
    got = [lax.ppermute(filter_spectrum, everyone, pairs[number]) for number in range(2)]
    ordered = [jnp.where(upper_zhi, got[1 - n], got[n]) for n in range(2)]
    mine = jnp.stack([jnp.where(odd, v[:, per_seq:], v[:, :per_seq]) for v in ordered])
    away = jnp.stack([jnp.where(odd, v[:, :per_seq], v[:, per_seq:]) for v in ordered])
    other = lax.ppermute(away, "y", near_y)
    mine, other = mine.reshape(2, half_row), other.reshape(2, half_row)
    filters = jnp.stack([jnp.where(odd, other, mine), jnp.where(odd, mine, other)])
    filters = doubling(filters, x_index >= 2, "x", far_x)
    filters = doubling(filters, x_index % 2 == 1, "x", near_x)
    filters = doubling(filters, upper_core, "core", cores).reshape(seq_count, half_row)

    tables = root_tables(positions)
    small_out = small_table(seq_count, False)
    small_back = small_table(seq_count, True)
    twiddle = jnp.asarray(np.stack(unit_roots(seq_count, positions, seq_count * positions)))

    core_flag = upper_core.astype(jnp.int32).reshape(1)
    wide = jax.ShapeDtypeStruct((seq_count, half_row), f32)
    part = jax.ShapeDtypeStruct((2, seq_count // 4, half_row), f32)
    rows = [pltpu.VMEM((4, 8 * seq_count, positions), bf16)]
    turned = [pltpu.VMEM((6 * seq_count, 2 * positions), bf16)]
    cost = pl.CostEstimate(flops=2 * 10**9, bytes_accessed=10**7, transcendentals=0)

    vmem = pl.BlockSpec(memory_space=pltpu.VMEM)
    spec, kept, away = pl.pallas_call(
        forward_kernel,
        out_shape=[wide, part, part],
        in_specs=[pl.BlockSpec(memory_space=pltpu.SMEM)] + [vmem] * 7,
        scratch_shapes=rows,
        name="forward",
        compiler_params=params,
        cost_estimate=cost,
    )(core_flag, moved, small_out, twiddle, *tables)

    total = kept + lax.ppermute(away, "core", cores)
    mine = jnp.where(odd, total[1], total[0])
    other = lax.ppermute(jnp.where(odd, total[0], total[1]), "y", near_y)
    total = jnp.stack([mine, other])
    total = halving(total, x_index % 2 == 1, "x", near_x)
    total = halving(total, x_index >= 2, "x", far_x)

    conv = pl.pallas_call(
        conv_kernel,
        out_shape=jax.ShapeDtypeStruct((seq_count, 2 * positions), f32),
        scratch_shapes=rows + turned,
        name="conv",
        compiler_params=params,
        cost_estimate=cost,
    )(moved, filters, small_back, twiddle, *tables)
    signals = pl.pallas_call(
        back_kernel,
        out_shape=jax.ShapeDtypeStruct((seq_count, 1, 4 * positions), f32),
        scratch_shapes=rows + turned,
        name="back",
        compiler_params=params,
        cost_estimate=cost,
    )(conv, spec, filters, small_back, twiddle, *tables)
    returned = lax.all_to_all(signals, SEQ, split_axis=0, concat_axis=0, tiled=True)
    returned = returned.reshape(seq_count, 4 * positions)

    ordered = jnp.where(odd, total[::-1], total)
    rows_out = [jnp.where(upper_zhi, ordered[:, 1 - n], ordered[:, n]) for n in range(2)]
    ends = [
        lax.ppermute(rows_out[number], everyone, [(b, a) for a, b in pairs[number]])
        for number in range(2)
    ]
    grad_filter = (
        (ends[0] + ends[1])
        .reshape(2, 2, per_seq, positions)
        .transpose(1, 0, 2, 3)
        .reshape(2, 2 * per_seq, positions)
    )

    scale = 1.0 / math.sqrt(seq_count * positions)
    conv = returned[:, : per_seq * positions].reshape(1, channels, positions) * scale
    backward = returned[:, per_seq * positions :].reshape(1, channels, positions) * scale
    grad_gate = (grad_out.astype(f32) * conv).astype(bf16)
    return (backward.astype(bf16), grad_gate, grad_filter)


def solution(mesh):
    split = Mesh(mesh.devices.reshape(2, 4, 2, 8, 4), DP + SEQ)
    return jax.shard_map(
        step,
        mesh=split,
        in_specs=(P(DP, None, SEQ), P(DP, None, SEQ), P(DP, None, None, SEQ), P(None, DP, SEQ)),
        out_specs=(P(DP, None, SEQ), P(DP, None, SEQ), P(None, DP, SEQ)),
        check_vma=False,
    )
```

```python
import math

import jax
import jax.numpy as jnp
import numpy as np
from jax import lax
from jax.experimental import pallas as pl
from jax.experimental.pallas import tpu as pltpu
from jax.sharding import Mesh, PartitionSpec as P


f32 = jnp.float32
bf16 = jnp.bfloat16
SEQ = ("zlo", "y")
DP = ("zhi", "x", "core")
MIB = 1024 * 1024


def unit_roots(rows, columns, period):
    product = np.outer(np.arange(rows, dtype=np.int64), np.arange(columns, dtype=np.int64))
    angle = (product % period).astype(np.float64) * (2.0 * np.pi / period)
    return np.cos(angle).astype(np.float32), np.sin(angle).astype(np.float32)


def halves(values):
    high = values.astype(bf16)
    return high, (values - high.astype(f32)).astype(bf16)


def three_terms(values, axis):
    high, low = halves(values)
    return jnp.concatenate([high, low, high], axis=axis)


def small_table(points, inverse):
    cosine, sine = unit_roots(points, points, points)
    whole = np.concatenate([cosine, -sine], axis=1 if inverse else 0)
    high = whole.astype(bf16)
    low = (whole - high.astype(np.float32)).astype(bf16)
    return jnp.asarray(np.concatenate([high, high, low], axis=1))


def dot16(left, right):
    return jnp.dot(left, right, preferred_element_type=f32)


def tables_kernel(coarse_ref, fine_ref, cos_hi, cos_lo, sin_hi, sin_lo):
    steps = fine_ref.shape[1]

    @pl.loop(0, coarse_ref.shape[1])
    def _(a):
        at = pl.ds(pl.multiple_of(a * steps, steps), steps)
        coarse_cos, coarse_sin = coarse_ref[0, pl.ds(a, 1), :], coarse_ref[1, pl.ds(a, 1), :]
        fine_cos, fine_sin = fine_ref[0], fine_ref[1]
        cosine = coarse_cos * fine_cos - coarse_sin * fine_sin
        sine = coarse_sin * fine_cos + coarse_cos * fine_sin
        cos_hi[at, :], cos_lo[at, :] = halves(cosine)
        sin_hi[at, :], sin_lo[at, :] = halves(sine)


def root_tables(points):
    steps, columns = 32, points // 4
    coarse = jnp.asarray(np.stack(unit_roots(points // steps, columns, points // steps)))
    fine = jnp.asarray(np.stack(unit_roots(steps, columns, points)))
    return pl.pallas_call(
        tables_kernel,
        out_shape=[jax.ShapeDtypeStruct((points, columns), bf16)] * 4,
        name="root_tables",
        compiler_params=pltpu.CompilerParams(vmem_limit_bytes=16 * MIB),
        cost_estimate=pl.CostEstimate(
            flops=20 * points * columns, bytes_accessed=8 * points * columns, transcendentals=0
        ),
    )(coarse, fine)


def keep_quarters(rows_ref, place, count, real, imag, conjugate):
    rows, points = real.shape
    lane = lax.broadcasted_iota(jnp.int32, (1, points), 1)
    odd = lane % 2 == 1
    alternate = jnp.where(odd, -1.0, 1.0)
    early = jnp.where(lane % 4 < 2, 1.0, -1.0)
    outer = jnp.where((lane + 1) % 4 < 2, 1.0, -1.0)
    swap_real, swap_imag = jnp.where(odd, imag, real), jnp.where(odd, real, imag)
    turned = [
        (real, imag),
        (swap_real * outer, swap_imag * early),
        (real * alternate, imag * alternate),
        (swap_real * early, swap_imag * outer),
    ]
    if conjugate:
        turned[1], turned[3] = turned[3], turned[1]
    for m in range(4):
        for part, values in enumerate(turned[m]):
            high, low = halves(values)
            first = (part * count + place) * rows
            rows_ref[m, first : first + rows, :] = high
            rows_ref[m, 2 * count * rows + first : 2 * count * rows + first + rows, :] = low


def root_product(high_low, hi_ref, lo_ref):
    rows = high_low.shape[0] // 2
    both = dot16(high_low, hi_ref[...])
    return both[:rows] + both[rows:] + dot16(high_low[:rows], lo_ref[...])


def pack_kernel(out_ref, gate_ref, spec_ref, packed_ref, rows_ref):
    points = out_ref.shape[2]
    count = packed_ref.shape[0]
    for source in range(3):
        for start in range(0, points, 128):
            cut = slice(start, start + 128)
            slot = source * (points // 128) + start // 128
            if source == 2:
                rows_ref[slot] = out_ref[0, :, cut].astype(f32) * gate_ref[0, :, cut].astype(f32)
            else:
                rows_ref[slot] = spec_ref[0, source, :, cut]
            for channel in range(2):
                at = (2 * source + channel) * points + start
                packed_ref[:, 0, at : at + 128] = rows_ref[slot, pl.ds(channel, count, stride=2), :]


def forward_kernel(
    core_ref, moved_ref, small_ref, twiddle_ref, cos_hi, cos_lo, sin_hi, sin_lo, spec_ref, kept_ref,
    away_ref, rows_ref,
):
    classes = moved_ref.shape[0]
    points = cos_hi.shape[0]
    scale = 1.0 / math.sqrt(classes * points)
    upper_core = core_ref[0] == 1
    quarter = classes // 4
    tw_cos, tw_sin = twiddle_ref[0] * scale, twiddle_ref[1] * scale
    for channel in range(2):
        delta = moved_ref[:, (4 + channel) * points : (5 + channel) * points]
        part = dot16(small_ref[...], three_terms(delta, 0))
        part_real, part_imag = part[:classes], part[classes:]
        turned_real = part_real * tw_cos + part_imag * tw_sin
        turned_imag = part_imag * tw_cos - part_real * tw_sin
        keep_quarters(rows_ref, channel, 2, turned_real, turned_imag, True)
    half = 2 * classes
    width = points // 4
    for tile in range(4):
        at = slice(tile * width, (tile + 1) * width)
        by_cos = root_product(rows_ref[tile], cos_hi, cos_lo)
        by_sin = root_product(rows_ref[tile], sin_hi, sin_lo)
        real = by_cos[:half] + by_sin[half:]
        imag = by_cos[half:] - by_sin[:half]
        for channel in range(2):
            mine = slice(channel * classes, (channel + 1) * classes)
            put_real = slice(channel * points + at.start, channel * points + at.stop)
            put_imag = slice((2 + channel) * points + at.start, (2 + channel) * points + at.stop)
            in_real, in_imag = moved_ref[:, put_real], moved_ref[:, put_imag]
            spec_ref[:, put_real] = real[mine]
            spec_ref[:, put_imag] = imag[mine]
            term_real = in_real * real[mine] + in_imag * imag[mine]
            term_imag = in_real * imag[mine] - in_imag * real[mine]
            for put, term in ((put_real, term_real), (put_imag, term_imag)):
                for side in range(2):
                    lower = term[2 * side * quarter : (2 * side + 1) * quarter]
                    upper = term[(2 * side + 1) * quarter : (2 * side + 2) * quarter]
                    kept_ref[side, :, put] = jnp.where(upper_core, upper, lower)
                    away_ref[side, :, put] = jnp.where(upper_core, lower, upper)


def inverse_rows(
    sign, odd_ref, first_ref, mine_ref, other_ref, small_ref, twiddle_ref, tables, rows_ref,
    turned_ref,
):
    cos_hi, cos_lo, sin_hi, sin_lo = tables
    classes = first_ref.shape[0]
    points = cos_hi.shape[0]
    odd = odd_ref[0] == 1

    def filt(at):
        mine, other = mine_ref[:, at], other_ref[:, at]
        return jnp.concatenate([jnp.where(odd, other, mine), jnp.where(odd, mine, other)], axis=0)

    for channel in range(2):
        real_at = slice(channel * points, (channel + 1) * points)
        imag_at = slice((2 + channel) * points, (3 + channel) * points)
        filt_real, filt_imag = filt(real_at), filt(imag_at) * sign
        first_real, first_imag = first_ref[:, real_at], first_ref[:, imag_at]
        keep_quarters(
            rows_ref,
            channel,
            2,
            first_real * filt_real - first_imag * filt_imag,
            first_real * filt_imag + first_imag * filt_real,
            False,
        )
    half = 2 * classes
    width = points // 4
    for tile in range(4):
        at = slice(tile * width, (tile + 1) * width)
        by_cos = root_product(rows_ref[tile], cos_hi, cos_lo)
        by_sin = root_product(rows_ref[tile], sin_hi, sin_lo)
        real = by_cos[:half] - by_sin[half:]
        imag = by_cos[half:] + by_sin[:half]
        tw_cos, tw_sin = twiddle_ref[0, :, at], twiddle_ref[1, :, at]
        for channel in range(2):
            mine = slice(channel * classes, (channel + 1) * classes)
            put = slice(channel * points + at.start, channel * points + at.stop)
            for part, turned in (
                (0, real[mine] * tw_cos - imag[mine] * tw_sin),
                (1, imag[mine] * tw_cos + real[mine] * tw_sin),
            ):
                high, low = halves(turned)
                for place, values in ((part, high), (2 + part, low), (4 + part, high)):
                    turned_ref[place * classes : (place + 1) * classes, put] = values
    return dot16(small_ref[...], turned_ref[...])


def conv_kernel(
    odd_ref, moved_ref, mine_ref, other_ref, small_ref, twiddle_ref, cos_hi, cos_lo, sin_hi, sin_lo,
    conv_ref, rows_ref, turned_ref,
):
    tables = (cos_hi, cos_lo, sin_hi, sin_lo)
    conv_ref[...] = inverse_rows(
        1.0, odd_ref, moved_ref, mine_ref, other_ref, small_ref, twiddle_ref, tables, rows_ref,
        turned_ref,
    )


def back_kernel(
    odd_ref, conv_ref, spec_ref, mine_ref, other_ref, small_ref, twiddle_ref, cos_hi, cos_lo,
    sin_hi, sin_lo, packed_ref, rows_ref, turned_ref,
):
    tables = (cos_hi, cos_lo, sin_hi, sin_lo)
    width = conv_ref.shape[1]
    packed_ref[:, 0, :width] = conv_ref[...]
    packed_ref[:, 0, width:] = inverse_rows(
        -1.0, odd_ref, spec_ref, mine_ref, other_ref, small_ref, twiddle_ref, tables, rows_ref,
        turned_ref,
    )


def staging_pairs(x_count, core_count, seq_count):
    pairs = []
    for number in range(2):
        found = []
        for d in range(2 * x_count * core_count):
            for s in range(seq_count):
                e0, core, near, far, e1 = [s >> bit & 1 for bit in (4, 3, 2, 1, 0)]
                row = ((e1 ^ number) * x_count + 2 * far + near) * core_count + core
                found.append((d * seq_count + s, row * seq_count + 2 * d + e0))
        pairs.append(found)
    return pairs


def kept_and_away(values, upper):
    half = values.shape[1] // 2
    lower, higher = values[:, :half], values[:, half:]
    return jnp.where(upper, higher, lower), jnp.where(upper, lower, higher)


def halving(values, upper, axis, pairs):
    kept, away = kept_and_away(values, upper)
    return kept + lax.ppermute(away, axis, pairs)


def doubling(values, upper, axis, pairs):
    other = lax.ppermute(values, axis, pairs)
    return jnp.concatenate(
        [jnp.where(upper, other, values), jnp.where(upper, values, other)], axis=0
    )


def step(grad_out, gate, input_spectrum, filter_spectrum):
    _, channels, positions = grad_out.shape
    seq_count = lax.axis_size(SEQ)
    x_count = lax.axis_size("x")
    everyone = DP + SEQ
    odd = lax.axis_index(SEQ) % 2 == 1
    upper_zhi = lax.axis_index("zhi") == 1
    upper_core = lax.axis_index("core") == 1
    x_index = lax.axis_index("x")
    pairs = staging_pairs(x_count, 2, seq_count)
    per_seq = channels // seq_count

    params = pltpu.CompilerParams(vmem_limit_bytes=16 * MIB)
    packed = pl.pallas_call(
        pack_kernel,
        out_shape=jax.ShapeDtypeStruct((seq_count, 1, 3 * per_seq * positions), f32),
        scratch_shapes=[pltpu.VMEM((3 * positions // 128, channels, 128), f32)],
        name="pack",
        compiler_params=params,
        cost_estimate=pl.CostEstimate(flops=10**5, bytes_accessed=2 * 10**6, transcendentals=0),
    )(grad_out, gate, input_spectrum)
    moved = lax.all_to_all(packed, SEQ, split_axis=0, concat_axis=0, tiled=True)
    moved = moved.reshape(seq_count, 3 * per_seq * positions)

    near_x = [(x, x ^ 1) for x in range(x_count)]
    far_x = [(x, x ^ 2) for x in range(x_count)]
    near_y = [(y, y ^ 1) for y in range(lax.axis_size("y"))]
    cores = [(0, 1), (1, 0)]
    half_row = 4 * positions
    got = [lax.ppermute(filter_spectrum, everyone, pairs[number]) for number in range(2)]
    filters = jnp.stack([jnp.where(upper_zhi, got[1 - n], got[n]) for n in range(2)])
    filters = (
        filters.reshape(2, 2, 2, per_seq, positions)
        .transpose(0, 2, 1, 3, 4)
        .reshape(2, 2 * half_row)
    )
    filters = doubling(filters, x_index >= 2, "x", far_x)
    filters = doubling(filters, x_index % 2 == 1, "x", near_x)
    filters = doubling(filters, upper_core, "core", cores)
    mine = jnp.where(odd, filters[:, half_row:], filters[:, :half_row])
    away = jnp.where(odd, filters[:, :half_row], filters[:, half_row:])
    filters = (mine, lax.ppermute(away, "y", near_y))

    tables = root_tables(positions)
    small_out = small_table(seq_count, False)
    small_back = small_table(seq_count, True)
    twiddle = jnp.asarray(np.stack(unit_roots(seq_count, positions, seq_count * positions)))

    core_flag = upper_core.astype(jnp.int32).reshape(1)
    wide = jax.ShapeDtypeStruct((seq_count, half_row), f32)
    part = jax.ShapeDtypeStruct((2, seq_count // 4, half_row), f32)
    rows = [pltpu.VMEM((4, 8 * seq_count, positions), bf16)]
    turned = [pltpu.VMEM((6 * seq_count, 2 * positions), bf16)]
    cost = pl.CostEstimate(flops=2 * 10**9, bytes_accessed=10**7, transcendentals=0)

    smem, vmem = pl.BlockSpec(memory_space=pltpu.SMEM), pl.BlockSpec(memory_space=pltpu.VMEM)
    parity = odd.astype(jnp.int32).reshape(1)
    spec, kept, away = pl.pallas_call(
        forward_kernel,
        out_shape=[wide, part, part],
        in_specs=[smem] + [vmem] * 7,
        scratch_shapes=rows,
        name="forward",
        compiler_params=params,
        cost_estimate=cost,
    )(core_flag, moved, small_out, twiddle, *tables)

    total = kept + lax.ppermute(away, "core", cores)
    mine = jnp.where(odd, total[1], total[0])
    other = lax.ppermute(jnp.where(odd, total[0], total[1]), "y", near_y)
    total = jnp.stack([mine, other])
    total = halving(total, x_index % 2 == 1, "x", near_x)
    total = halving(total, x_index >= 2, "x", far_x)

    conv = pl.pallas_call(
        conv_kernel,
        out_shape=jax.ShapeDtypeStruct((seq_count, 2 * positions), f32),
        scratch_shapes=rows + turned,
        in_specs=[smem] + [vmem] * 9,
        name="conv",
        compiler_params=params,
        cost_estimate=cost,
    )(parity, moved, *filters, small_back, twiddle, *tables)
    signals = pl.pallas_call(
        back_kernel,
        out_shape=jax.ShapeDtypeStruct((seq_count, 1, 4 * positions), f32),
        scratch_shapes=rows + turned,
        in_specs=[smem] + [vmem] * 10,
        name="back",
        compiler_params=params,
        cost_estimate=cost,
    )(parity, conv, spec, *filters, small_back, twiddle, *tables)
    returned = lax.all_to_all(signals, SEQ, split_axis=0, concat_axis=0, tiled=True)
    returned = returned.reshape(seq_count, 4 * positions)

    ordered = jnp.where(odd, total[::-1], total)
    rows_out = [jnp.where(upper_zhi, ordered[:, 1 - n], ordered[:, n]) for n in range(2)]
    ends = [
        lax.ppermute(rows_out[number], everyone, [(b, a) for a, b in pairs[number]])
        for number in range(2)
    ]
    grad_filter = (
        (ends[0] + ends[1])
        .reshape(2, 2, per_seq, positions)
        .transpose(1, 0, 2, 3)
        .reshape(2, 2 * per_seq, positions)
    )

    scale = 1.0 / math.sqrt(seq_count * positions)
    conv = returned[:, : per_seq * positions].reshape(1, channels, positions) * scale
    backward = returned[:, per_seq * positions :].reshape(1, channels, positions) * scale
    grad_gate = (grad_out.astype(f32) * conv).astype(bf16)
    return (backward.astype(bf16), grad_gate, grad_filter)


def solution(mesh):
    split = Mesh(mesh.devices.reshape(2, 4, 2, 8, 4), DP + SEQ)
    return jax.shard_map(
        step,
        mesh=split,
        in_specs=(P(DP, None, SEQ), P(DP, None, SEQ), P(DP, None, None, SEQ), P(None, DP, SEQ)),
        out_specs=(P(DP, None, SEQ), P(DP, None, SEQ), P(None, DP, SEQ)),
        check_vma=False,
    )
```

```python
import math

import jax
import jax.numpy as jnp
import numpy as np
from jax import lax
from jax.experimental import pallas as pl
from jax.experimental.pallas import tpu as pltpu
from jax.sharding import Mesh, PartitionSpec as P


f32 = jnp.float32
bf16 = jnp.bfloat16
SEQ = ("zlo", "y")
DP = ("zhi", "x", "core")
MIB = 1024 * 1024


def unit_roots(rows, columns, period):
    product = np.outer(np.arange(rows, dtype=np.int64), np.arange(columns, dtype=np.int64))
    angle = (product % period).astype(np.float64) * (2.0 * np.pi / period)
    return np.cos(angle).astype(np.float32), np.sin(angle).astype(np.float32)


def halves(values):
    high = values.astype(bf16)
    return high, (values - high.astype(f32)).astype(bf16)


def three_terms(values, axis):
    high, low = halves(values)
    return jnp.concatenate([high, low, high], axis=axis)


def small_table(points, inverse):
    cosine, sine = unit_roots(points, points, points)
    whole = np.concatenate([cosine, -sine], axis=1 if inverse else 0)
    high = whole.astype(bf16)
    low = (whole - high.astype(np.float32)).astype(bf16)
    return jnp.asarray(np.concatenate([high, high, low], axis=1))


def dot16(left, right):
    return jnp.dot(left, right, preferred_element_type=f32)


def tables_kernel(coarse_ref, fine_ref, cos_hi, cos_lo, sin_hi, sin_lo):
    steps = fine_ref.shape[1]

    @pl.loop(0, coarse_ref.shape[1])
    def _(a):
        at = pl.ds(pl.multiple_of(a * steps, steps), steps)
        coarse_cos, coarse_sin = coarse_ref[0, pl.ds(a, 1), :], coarse_ref[1, pl.ds(a, 1), :]
        fine_cos, fine_sin = fine_ref[0], fine_ref[1]
        cosine = coarse_cos * fine_cos - coarse_sin * fine_sin
        sine = coarse_sin * fine_cos + coarse_cos * fine_sin
        cos_hi[at, :], cos_lo[at, :] = halves(cosine)
        sin_hi[at, :], sin_lo[at, :] = halves(sine)


def root_tables(points):
    steps, columns = 32, points // 4
    coarse = jnp.asarray(np.stack(unit_roots(points // steps, columns, points // steps)))
    fine = jnp.asarray(np.stack(unit_roots(steps, columns, points)))
    return pl.pallas_call(
        tables_kernel,
        out_shape=[jax.ShapeDtypeStruct((points, columns), bf16)] * 4,
        name="root_tables",
        compiler_params=pltpu.CompilerParams(vmem_limit_bytes=16 * MIB),
        cost_estimate=pl.CostEstimate(
            flops=20 * points * columns, bytes_accessed=8 * points * columns, transcendentals=0
        ),
    )(coarse, fine)


def keep_quarters(rows_ref, place, count, real, imag, conjugate):
    rows, points = real.shape
    lane = lax.broadcasted_iota(jnp.int32, (1, points), 1)
    odd = lane % 2 == 1
    alternate = jnp.where(odd, -1.0, 1.0)
    early = jnp.where(lane % 4 < 2, 1.0, -1.0)
    outer = jnp.where((lane + 1) % 4 < 2, 1.0, -1.0)
    swap_real, swap_imag = jnp.where(odd, imag, real), jnp.where(odd, real, imag)
    turned = [
        (real, imag),
        (swap_real * outer, swap_imag * early),
        (real * alternate, imag * alternate),
        (swap_real * early, swap_imag * outer),
    ]
    if conjugate:
        turned[1], turned[3] = turned[3], turned[1]
    for m in range(4):
        for part, values in enumerate(turned[m]):
            high, low = halves(values)
            first = (part * count + place) * rows
            rows_ref[m, first : first + rows, :] = high
            rows_ref[m, 2 * count * rows + first : 2 * count * rows + first + rows, :] = low


def root_product(high_low, hi_ref, lo_ref):
    rows = high_low.shape[0] // 2
    both = dot16(high_low, hi_ref[...])
    return both[:rows] + both[rows:] + dot16(high_low[:rows], lo_ref[...])


def pack_kernel(out_ref, gate_ref, spec_ref, packed_ref, rows_ref):
    points = out_ref.shape[2]
    count = packed_ref.shape[0]
    for source in range(3):
        for start in range(0, points, 128):
            cut = slice(start, start + 128)
            slot = source * (points // 128) + start // 128
            if source == 2:
                rows_ref[slot] = out_ref[0, :, cut].astype(f32) * gate_ref[0, :, cut].astype(f32)
            else:
                rows_ref[slot] = spec_ref[0, source, :, cut]
            for channel in range(2):
                at = (2 * source + channel) * points + start
                packed_ref[:, 0, at : at + 128] = rows_ref[slot, pl.ds(channel, count, stride=2), :]


def forward_kernel(
    core_ref, moved_ref, small_ref, twiddle_ref, cos_hi, cos_lo, sin_hi, sin_lo, spec_ref, kept_ref,
    away_ref, rows_ref,
):
    classes = moved_ref.shape[0]
    points = cos_hi.shape[0]
    scale = 1.0 / math.sqrt(classes * points)
    upper_core = core_ref[0] == 1
    quarter = classes // 4
    tw_cos, tw_sin = twiddle_ref[0] * scale, twiddle_ref[1] * scale
    for channel in range(2):
        delta = moved_ref[:, (4 + channel) * points : (5 + channel) * points]
        part = dot16(small_ref[...], three_terms(delta, 0))
        part_real, part_imag = part[:classes], part[classes:]
        turned_real = part_real * tw_cos + part_imag * tw_sin
        turned_imag = part_imag * tw_cos - part_real * tw_sin
        keep_quarters(rows_ref, channel, 2, turned_real, turned_imag, True)
    half = 2 * classes
    width = points // 4
    for tile in range(4):
        at = slice(tile * width, (tile + 1) * width)
        by_cos = root_product(rows_ref[tile], cos_hi, cos_lo)
        by_sin = root_product(rows_ref[tile], sin_hi, sin_lo)
        real = by_cos[:half] + by_sin[half:]
        imag = by_cos[half:] - by_sin[:half]
        for channel in range(2):
            mine = slice(channel * classes, (channel + 1) * classes)
            put_real = slice(channel * points + at.start, channel * points + at.stop)
            put_imag = slice((2 + channel) * points + at.start, (2 + channel) * points + at.stop)
            in_real, in_imag = moved_ref[:, put_real], moved_ref[:, put_imag]
            spec_ref[:, put_real] = real[mine]
            spec_ref[:, put_imag] = imag[mine]
            term_real = in_real * real[mine] + in_imag * imag[mine]
            term_imag = in_real * imag[mine] - in_imag * real[mine]
            for put, term in ((put_real, term_real), (put_imag, term_imag)):
                for side in range(2):
                    lower = term[2 * side * quarter : (2 * side + 1) * quarter]
                    upper = term[(2 * side + 1) * quarter : (2 * side + 2) * quarter]
                    kept_ref[side, :, put] = jnp.where(upper_core, upper, lower)
                    away_ref[side, :, put] = jnp.where(upper_core, lower, upper)


def inverse_rows(
    sign, first_ref, filt_ref, small_ref, twiddle_ref, tables, rows_ref, turned_ref
):
    cos_hi, cos_lo, sin_hi, sin_lo = tables
    classes = first_ref.shape[0]
    points = cos_hi.shape[0]
    for channel in range(2):
        real_at = slice(channel * points, (channel + 1) * points)
        imag_at = slice((2 + channel) * points, (3 + channel) * points)
        filt_real, filt_imag = filt_ref[:, real_at], filt_ref[:, imag_at] * sign
        first_real, first_imag = first_ref[:, real_at], first_ref[:, imag_at]
        keep_quarters(
            rows_ref,
            channel,
            2,
            first_real * filt_real - first_imag * filt_imag,
            first_real * filt_imag + first_imag * filt_real,
            False,
        )
    half = 2 * classes
    width = points // 4
    for tile in range(4):
        at = slice(tile * width, (tile + 1) * width)
        by_cos = root_product(rows_ref[tile], cos_hi, cos_lo)
        by_sin = root_product(rows_ref[tile], sin_hi, sin_lo)
        real = by_cos[:half] - by_sin[half:]
        imag = by_cos[half:] + by_sin[:half]
        tw_cos, tw_sin = twiddle_ref[0, :, at], twiddle_ref[1, :, at]
        for channel in range(2):
            mine = slice(channel * classes, (channel + 1) * classes)
            put = slice(channel * points + at.start, channel * points + at.stop)
            for part, turned in (
                (0, real[mine] * tw_cos - imag[mine] * tw_sin),
                (1, imag[mine] * tw_cos + real[mine] * tw_sin),
            ):
                high, low = halves(turned)
                for place, values in ((part, high), (2 + part, low), (4 + part, high)):
                    turned_ref[place * classes : (place + 1) * classes, put] = values
    return dot16(small_ref[...], turned_ref[...])


def conv_kernel(
    moved_ref, filt_ref, small_ref, twiddle_ref, cos_hi, cos_lo, sin_hi, sin_lo, packed_ref, rows_ref,
    turned_ref,
):
    tables = (cos_hi, cos_lo, sin_hi, sin_lo)
    packed_ref[:, 0, :] = inverse_rows(
        1.0, moved_ref, filt_ref, small_ref, twiddle_ref, tables, rows_ref, turned_ref
    )


def back_kernel(
    spec_ref, filt_ref, small_ref, twiddle_ref, cos_hi, cos_lo, sin_hi, sin_lo, packed_ref, rows_ref,
    turned_ref,
):
    tables = (cos_hi, cos_lo, sin_hi, sin_lo)
    packed_ref[:, 0, :] = inverse_rows(
        -1.0, spec_ref, filt_ref, small_ref, twiddle_ref, tables, rows_ref, turned_ref
    )


def staging_pairs(x_count, core_count, seq_count):
    pairs = []
    for number in range(2):
        found = []
        for d in range(2 * x_count * core_count):
            for s in range(seq_count):
                e0, core, near, far, e1 = [s >> bit & 1 for bit in (4, 3, 2, 1, 0)]
                row = ((e1 ^ number) * x_count + 2 * far + near) * core_count + core
                found.append((d * seq_count + s, row * seq_count + 2 * d + e0))
        pairs.append(found)
    return pairs


def kept_and_away(values, upper):
    half = values.shape[1] // 2
    lower, higher = values[:, :half], values[:, half:]
    return jnp.where(upper, higher, lower), jnp.where(upper, lower, higher)


def halving(values, upper, axis, pairs):
    kept, away = kept_and_away(values, upper)
    return kept + lax.ppermute(away, axis, pairs)


def doubling(values, upper, axis, pairs):
    other = lax.ppermute(values, axis, pairs)
    return jnp.concatenate(
        [jnp.where(upper, other, values), jnp.where(upper, values, other)], axis=1
    )


def step(grad_out, gate, input_spectrum, filter_spectrum):
    _, channels, positions = grad_out.shape
    seq_count = lax.axis_size(SEQ)
    x_count = lax.axis_size("x")
    everyone = DP + SEQ
    odd = lax.axis_index(SEQ) % 2 == 1
    upper_zhi = lax.axis_index("zhi") == 1
    upper_core = lax.axis_index("core") == 1
    x_index = lax.axis_index("x")
    pairs = staging_pairs(x_count, 2, seq_count)
    per_seq = channels // seq_count

    params = pltpu.CompilerParams(vmem_limit_bytes=16 * MIB)
    packed = pl.pallas_call(
        pack_kernel,
        out_shape=jax.ShapeDtypeStruct((seq_count, 1, 3 * per_seq * positions), f32),
        scratch_shapes=[pltpu.VMEM((3 * positions // 128, channels, 128), f32)],
        name="pack",
        compiler_params=params,
        cost_estimate=pl.CostEstimate(flops=10**5, bytes_accessed=2 * 10**6, transcendentals=0),
    )(grad_out, gate, input_spectrum)
    moved = lax.all_to_all(packed, SEQ, split_axis=0, concat_axis=0, tiled=True)
    moved = moved.reshape(seq_count, 3 * per_seq * positions)

    near_x = [(x, x ^ 1) for x in range(x_count)]
    far_x = [(x, x ^ 2) for x in range(x_count)]
    near_y = [(y, y ^ 1) for y in range(lax.axis_size("y"))]
    cores = [(0, 1), (1, 0)]
    half_row = 4 * positions
    got = [lax.ppermute(filter_spectrum, everyone, pairs[number]) for number in range(2)]
    ordered = [jnp.where(upper_zhi, got[1 - n], got[n]) for n in range(2)]
    mine = jnp.stack([jnp.where(odd, v[:, per_seq:], v[:, :per_seq]) for v in ordered])
    away = jnp.stack([jnp.where(odd, v[:, :per_seq], v[:, per_seq:]) for v in ordered])
    other = lax.ppermute(away, "y", near_y)
    mine, other = mine.reshape(2, half_row), other.reshape(2, half_row)
    filters = jnp.stack([jnp.where(odd, other, mine), jnp.where(odd, mine, other)])
    filters = doubling(filters, x_index >= 2, "x", far_x)
    filters = doubling(filters, x_index % 2 == 1, "x", near_x)
    filters = doubling(filters, upper_core, "core", cores).reshape(seq_count, half_row)

    tables = root_tables(positions)
    small_out = small_table(seq_count, False)
    small_back = small_table(seq_count, True)
    twiddle = jnp.asarray(np.stack(unit_roots(seq_count, positions, seq_count * positions)))

    core_flag = upper_core.astype(jnp.int32).reshape(1)
    wide = jax.ShapeDtypeStruct((seq_count, half_row), f32)
    part = jax.ShapeDtypeStruct((2, seq_count // 4, half_row), f32)
    rows = [pltpu.VMEM((4, 8 * seq_count, positions), bf16)]
    turned = [pltpu.VMEM((6 * seq_count, 2 * positions), bf16)]
    cost = pl.CostEstimate(flops=2 * 10**9, bytes_accessed=10**7, transcendentals=0)

    vmem = pl.BlockSpec(memory_space=pltpu.VMEM)
    spec, kept, away = pl.pallas_call(
        forward_kernel,
        out_shape=[wide, part, part],
        in_specs=[pl.BlockSpec(memory_space=pltpu.SMEM)] + [vmem] * 7,
        scratch_shapes=rows,
        name="forward",
        compiler_params=params,
        cost_estimate=cost,
    )(core_flag, moved, small_out, twiddle, *tables)

    total = kept + lax.ppermute(away, "core", cores)
    mine = jnp.where(odd, total[1], total[0])
    other = lax.ppermute(jnp.where(odd, total[0], total[1]), "y", near_y)
    total = jnp.stack([mine, other])
    total = halving(total, x_index % 2 == 1, "x", near_x)
    total = halving(total, x_index >= 2, "x", far_x)

    signal = jax.ShapeDtypeStruct((seq_count, 1, per_seq * positions), f32)

    def inverse(kernel, first):
        return pl.pallas_call(
            kernel,
            out_shape=signal,
            scratch_shapes=rows + turned,
            compiler_params=params,
            cost_estimate=cost,
        )(first, filters, small_back, twiddle, *tables)

    signals = inverse(conv_kernel, moved)
    conv = lax.all_to_all(signals, SEQ, split_axis=0, concat_axis=0, tiled=True)
    signals = inverse(back_kernel, spec)
    back = lax.all_to_all(signals, SEQ, split_axis=0, concat_axis=0, tiled=True)

    ordered = jnp.where(odd, total[::-1], total)
    rows_out = [jnp.where(upper_zhi, ordered[:, 1 - n], ordered[:, n]) for n in range(2)]
    ends = [
        lax.ppermute(rows_out[number], everyone, [(b, a) for a, b in pairs[number]])
        for number in range(2)
    ]
    grad_filter = (
        (ends[0] + ends[1])
        .reshape(2, 2, per_seq, positions)
        .transpose(1, 0, 2, 3)
        .reshape(2, 2 * per_seq, positions)
    )

    scale = 1.0 / math.sqrt(seq_count * positions)
    conv = conv.reshape(1, channels, positions) * scale
    backward = back.reshape(1, channels, positions) * scale
    grad_gate = (grad_out.astype(f32) * conv).astype(bf16)
    return (backward.astype(bf16), grad_gate, grad_filter)


def solution(mesh):
    split = Mesh(mesh.devices.reshape(2, 4, 2, 8, 4), DP + SEQ)
    return jax.shard_map(
        step,
        mesh=split,
        in_specs=(P(DP, None, SEQ), P(DP, None, SEQ), P(DP, None, None, SEQ), P(None, DP, SEQ)),
        out_specs=(P(DP, None, SEQ), P(DP, None, SEQ), P(None, DP, SEQ)),
        check_vma=False,
    )
```

```python
import math

import jax
import jax.numpy as jnp
import numpy as np
from jax import lax
from jax.experimental import pallas as pl
from jax.experimental.pallas import tpu as pltpu
from jax.sharding import Mesh, PartitionSpec as P


f32 = jnp.float32
bf16 = jnp.bfloat16
SEQ = ("zlo", "y")
DP = ("zhi", "x", "core")
MIB = 1024 * 1024


def unit_roots(rows, columns, period):
    product = np.outer(np.arange(rows, dtype=np.int64), np.arange(columns, dtype=np.int64))
    angle = (product % period).astype(np.float64) * (2.0 * np.pi / period)
    return np.cos(angle).astype(np.float32), np.sin(angle).astype(np.float32)


def halves(values):
    high = values.astype(bf16)
    return high, (values - high.astype(f32)).astype(bf16)


def three_terms(values, axis):
    high, low = halves(values)
    return jnp.concatenate([high, low, high], axis=axis)


def small_table(points, inverse):
    cosine, sine = unit_roots(points, points, points)
    whole = np.concatenate([cosine, -sine], axis=1 if inverse else 0)
    high = whole.astype(bf16)
    low = (whole - high.astype(np.float32)).astype(bf16)
    return jnp.asarray(np.concatenate([high, high, low], axis=1))


def dot16(left, right):
    return jnp.dot(left, right, preferred_element_type=f32)


def tables_kernel(coarse_ref, fine_ref, cos_hi, cos_lo, sin_hi, sin_lo):
    steps = fine_ref.shape[1]

    @pl.loop(0, coarse_ref.shape[1])
    def _(a):
        at = pl.ds(pl.multiple_of(a * steps, steps), steps)
        coarse_cos, coarse_sin = coarse_ref[0, pl.ds(a, 1), :], coarse_ref[1, pl.ds(a, 1), :]
        fine_cos, fine_sin = fine_ref[0], fine_ref[1]
        cosine = coarse_cos * fine_cos - coarse_sin * fine_sin
        sine = coarse_sin * fine_cos + coarse_cos * fine_sin
        cos_hi[at, :], cos_lo[at, :] = halves(cosine)
        sin_hi[at, :], sin_lo[at, :] = halves(sine)


def root_tables(points):
    steps, columns = 32, points // 4
    coarse = jnp.asarray(np.stack(unit_roots(points // steps, columns, points // steps)))
    fine = jnp.asarray(np.stack(unit_roots(steps, columns, points)))
    return pl.pallas_call(
        tables_kernel,
        out_shape=[jax.ShapeDtypeStruct((points, columns), bf16)] * 4,
        name="root_tables",
        compiler_params=pltpu.CompilerParams(vmem_limit_bytes=16 * MIB),
        cost_estimate=pl.CostEstimate(
            flops=20 * points * columns, bytes_accessed=8 * points * columns, transcendentals=0
        ),
    )(coarse, fine)


def keep_quarters(rows_ref, place, count, real, imag, conjugate):
    rows, points = real.shape
    lane = lax.broadcasted_iota(jnp.int32, (1, points), 1)
    odd = lane % 2 == 1
    alternate = jnp.where(odd, -1.0, 1.0)
    early = jnp.where(lane % 4 < 2, 1.0, -1.0)
    outer = jnp.where((lane + 1) % 4 < 2, 1.0, -1.0)
    swap_real, swap_imag = jnp.where(odd, imag, real), jnp.where(odd, real, imag)
    turned = [
        (real, imag),
        (swap_real * outer, swap_imag * early),
        (real * alternate, imag * alternate),
        (swap_real * early, swap_imag * outer),
    ]
    if conjugate:
        turned[1], turned[3] = turned[3], turned[1]
    for m in range(4):
        for part, values in enumerate(turned[m]):
            high, low = halves(values)
            first = (part * count + place) * rows
            rows_ref[m, first : first + rows, :] = high
            rows_ref[m, 2 * count * rows + first : 2 * count * rows + first + rows, :] = low


def root_product(high_low, hi_ref, lo_ref):
    rows = high_low.shape[0] // 2
    both = dot16(high_low, hi_ref[...])
    return both[:rows] + both[rows:] + dot16(high_low[:rows], lo_ref[...])


def pack_kernel(
    out_hbm, gate_hbm, spec_hbm, packed_ref, out_ref, gate_ref, spec_ref, rows_ref, semaphores
):
    copies = [
        pltpu.make_async_copy(spec_hbm.at[0, 0], spec_ref.at[0], semaphores.at[0]),
        pltpu.make_async_copy(spec_hbm.at[0, 1], spec_ref.at[1], semaphores.at[1]),
        pltpu.make_async_copy(out_hbm.at[0], out_ref, semaphores.at[2]),
        pltpu.make_async_copy(gate_hbm.at[0], gate_ref, semaphores.at[3]),
    ]
    for copy in copies:
        copy.start()
    points = out_ref.shape[1]
    count = packed_ref.shape[0]
    for source in range(3):
        copies[source].wait()
        if source == 2:
            copies[3].wait()
        for start in range(0, points, 128):
            cut = slice(start, start + 128)
            slot = source * (points // 128) + start // 128
            if source == 2:
                rows_ref[slot] = out_ref[:, cut].astype(f32) * gate_ref[:, cut].astype(f32)
            else:
                rows_ref[slot] = spec_ref[source, :, cut]
            for channel in range(2):
                at = (2 * source + channel) * points + start
                packed_ref[:, 0, at : at + 128] = rows_ref[slot, pl.ds(channel, count, stride=2), :]


def forward_kernel(
    core_ref, moved_ref, small_ref, twiddle_ref, cos_hi, cos_lo, sin_hi, sin_lo, spec_ref, kept_ref,
    away_ref, rows_ref,
):
    classes = moved_ref.shape[0]
    points = cos_hi.shape[0]
    scale = 1.0 / math.sqrt(classes * points)
    upper_core = core_ref[0] == 1
    quarter = classes // 4
    tw_cos, tw_sin = twiddle_ref[0] * scale, twiddle_ref[1] * scale
    for channel in range(2):
        delta = moved_ref[:, (4 + channel) * points : (5 + channel) * points]
        part = dot16(small_ref[...], three_terms(delta, 0))
        part_real, part_imag = part[:classes], part[classes:]
        turned_real = part_real * tw_cos + part_imag * tw_sin
        turned_imag = part_imag * tw_cos - part_real * tw_sin
        keep_quarters(rows_ref, channel, 2, turned_real, turned_imag, True)
    half = 2 * classes
    width = points // 4
    for tile in range(4):
        at = slice(tile * width, (tile + 1) * width)
        by_cos = root_product(rows_ref[tile], cos_hi, cos_lo)
        by_sin = root_product(rows_ref[tile], sin_hi, sin_lo)
        real = by_cos[:half] + by_sin[half:]
        imag = by_cos[half:] - by_sin[:half]
        for channel in range(2):
            mine = slice(channel * classes, (channel + 1) * classes)
            put_real = slice(channel * points + at.start, channel * points + at.stop)
            put_imag = slice((2 + channel) * points + at.start, (2 + channel) * points + at.stop)
            in_real, in_imag = moved_ref[:, put_real], moved_ref[:, put_imag]
            spec_ref[:, put_real] = real[mine]
            spec_ref[:, put_imag] = imag[mine]
            term_real = in_real * real[mine] + in_imag * imag[mine]
            term_imag = in_real * imag[mine] - in_imag * real[mine]
            for put, term in ((put_real, term_real), (put_imag, term_imag)):
                for side in range(2):
                    lower = term[2 * side * quarter : (2 * side + 1) * quarter]
                    upper = term[(2 * side + 1) * quarter : (2 * side + 2) * quarter]
                    kept_ref[side, :, put] = jnp.where(upper_core, upper, lower)
                    away_ref[side, :, put] = jnp.where(upper_core, lower, upper)


def inverse_rows(
    sign, first_ref, filt_ref, small_ref, twiddle_ref, tables, rows_ref, turned_ref
):
    cos_hi, cos_lo, sin_hi, sin_lo = tables
    classes = first_ref.shape[0]
    points = cos_hi.shape[0]
    for channel in range(2):
        real_at = slice(channel * points, (channel + 1) * points)
        imag_at = slice((2 + channel) * points, (3 + channel) * points)
        filt_real, filt_imag = filt_ref[:, real_at], filt_ref[:, imag_at] * sign
        first_real, first_imag = first_ref[:, real_at], first_ref[:, imag_at]
        keep_quarters(
            rows_ref,
            channel,
            2,
            first_real * filt_real - first_imag * filt_imag,
            first_real * filt_imag + first_imag * filt_real,
            False,
        )
    half = 2 * classes
    width = points // 4
    for tile in range(4):
        at = slice(tile * width, (tile + 1) * width)
        by_cos = root_product(rows_ref[tile], cos_hi, cos_lo)
        by_sin = root_product(rows_ref[tile], sin_hi, sin_lo)
        real = by_cos[:half] - by_sin[half:]
        imag = by_cos[half:] + by_sin[:half]
        tw_cos, tw_sin = twiddle_ref[0, :, at], twiddle_ref[1, :, at]
        for channel in range(2):
            mine = slice(channel * classes, (channel + 1) * classes)
            put = slice(channel * points + at.start, channel * points + at.stop)
            for part, turned in (
                (0, real[mine] * tw_cos - imag[mine] * tw_sin),
                (1, imag[mine] * tw_cos + real[mine] * tw_sin),
            ):
                high, low = halves(turned)
                for place, values in ((part, high), (2 + part, low), (4 + part, high)):
                    turned_ref[place * classes : (place + 1) * classes, put] = values
    return dot16(small_ref[...], turned_ref[...])


def conv_kernel(
    moved_ref, filt_ref, small_ref, twiddle_ref, cos_hi, cos_lo, sin_hi, sin_lo, conv_ref, rows_ref,
    turned_ref,
):
    tables = (cos_hi, cos_lo, sin_hi, sin_lo)
    conv_ref[...] = inverse_rows(
        1.0, moved_ref, filt_ref, small_ref, twiddle_ref, tables, rows_ref, turned_ref
    )


def back_kernel(
    conv_ref, spec_ref, filt_ref, small_ref, twiddle_ref, cos_hi, cos_lo, sin_hi, sin_lo, packed_ref,
    rows_ref, turned_ref,
):
    tables = (cos_hi, cos_lo, sin_hi, sin_lo)
    width = conv_ref.shape[1]
    packed_ref[:, 0, :width] = conv_ref[...]
    packed_ref[:, 0, width:] = inverse_rows(
        -1.0, spec_ref, filt_ref, small_ref, twiddle_ref, tables, rows_ref, turned_ref
    )


def staging_pairs(x_count, core_count, seq_count):
    pairs = []
    for number in range(2):
        found = []
        for d in range(2 * x_count * core_count):
            for s in range(seq_count):
                e0, core, near, far, e1 = [s >> bit & 1 for bit in (4, 3, 2, 1, 0)]
                row = ((e1 ^ number) * x_count + 2 * far + near) * core_count + core
                found.append((d * seq_count + s, row * seq_count + 2 * d + e0))
        pairs.append(found)
    return pairs


def kept_and_away(values, upper):
    half = values.shape[1] // 2
    lower, higher = values[:, :half], values[:, half:]
    return jnp.where(upper, higher, lower), jnp.where(upper, lower, higher)


def halving(values, upper, axis, pairs):
    kept, away = kept_and_away(values, upper)
    return kept + lax.ppermute(away, axis, pairs)


def doubling(values, upper, axis, pairs):
    other = lax.ppermute(values, axis, pairs)
    return jnp.concatenate(
        [jnp.where(upper, other, values), jnp.where(upper, values, other)], axis=1
    )


def step(grad_out, gate, input_spectrum, filter_spectrum):
    _, channels, positions = grad_out.shape
    seq_count = lax.axis_size(SEQ)
    x_count = lax.axis_size("x")
    everyone = DP + SEQ
    odd = lax.axis_index(SEQ) % 2 == 1
    upper_zhi = lax.axis_index("zhi") == 1
    upper_core = lax.axis_index("core") == 1
    x_index = lax.axis_index("x")
    pairs = staging_pairs(x_count, 2, seq_count)
    per_seq = channels // seq_count

    params = pltpu.CompilerParams(vmem_limit_bytes=16 * MIB)
    packed = pl.pallas_call(
        pack_kernel,
        out_shape=jax.ShapeDtypeStruct((seq_count, 1, 3 * per_seq * positions), f32),
        in_specs=[pl.BlockSpec(memory_space=pltpu.HBM)] * 3,
        scratch_shapes=[
            pltpu.VMEM((channels, positions), bf16),
            pltpu.VMEM((channels, positions), bf16),
            pltpu.VMEM((2, channels, positions), f32),
            pltpu.VMEM((3 * positions // 128, channels, 128), f32),
            pltpu.SemaphoreType.DMA((4,)),
        ],
        name="pack",
        compiler_params=pltpu.CompilerParams(vmem_limit_bytes=63 * MIB),
        cost_estimate=pl.CostEstimate(flops=10**5, bytes_accessed=2 * 10**6, transcendentals=0),
    )(grad_out, gate, input_spectrum)
    moved = lax.all_to_all(packed, SEQ, split_axis=0, concat_axis=0, tiled=True)
    moved = moved.reshape(seq_count, 3 * per_seq * positions)

    near_x = [(x, x ^ 1) for x in range(x_count)]
    far_x = [(x, x ^ 2) for x in range(x_count)]
    near_y = [(y, y ^ 1) for y in range(lax.axis_size("y"))]
    cores = [(0, 1), (1, 0)]
    half_row = 4 * positions
    got = [lax.ppermute(filter_spectrum, everyone, pairs[number]) for number in range(2)]
    ordered = [jnp.where(upper_zhi, got[1 - n], got[n]) for n in range(2)]
    mine = jnp.stack([jnp.where(odd, v[:, per_seq:], v[:, :per_seq]) for v in ordered])
    away = jnp.stack([jnp.where(odd, v[:, :per_seq], v[:, per_seq:]) for v in ordered])
    other = lax.ppermute(away, "y", near_y)
    mine, other = mine.reshape(2, half_row), other.reshape(2, half_row)
    filters = jnp.stack([jnp.where(odd, other, mine), jnp.where(odd, mine, other)])
    filters = doubling(filters, x_index >= 2, "x", far_x)
    filters = doubling(filters, x_index % 2 == 1, "x", near_x)
    filters = doubling(filters, upper_core, "core", cores).reshape(seq_count, half_row)

    tables = root_tables(positions)
    small_out = small_table(seq_count, False)
    small_back = small_table(seq_count, True)
    twiddle = jnp.asarray(np.stack(unit_roots(seq_count, positions, seq_count * positions)))

    core_flag = upper_core.astype(jnp.int32).reshape(1)
    wide = jax.ShapeDtypeStruct((seq_count, half_row), f32)
    part = jax.ShapeDtypeStruct((2, seq_count // 4, half_row), f32)
    rows = [pltpu.VMEM((4, 8 * seq_count, positions), bf16)]
    turned = [pltpu.VMEM((6 * seq_count, 2 * positions), bf16)]
    cost = pl.CostEstimate(flops=2 * 10**9, bytes_accessed=10**7, transcendentals=0)

    vmem = pl.BlockSpec(memory_space=pltpu.VMEM)
    spec, kept, away = pl.pallas_call(
        forward_kernel,
        out_shape=[wide, part, part],
        in_specs=[pl.BlockSpec(memory_space=pltpu.SMEM)] + [vmem] * 7,
        scratch_shapes=rows,
        name="forward",
        compiler_params=params,
        cost_estimate=cost,
    )(core_flag, moved, small_out, twiddle, *tables)

    total = kept + lax.ppermute(away, "core", cores)
    mine = jnp.where(odd, total[1], total[0])
    other = lax.ppermute(jnp.where(odd, total[0], total[1]), "y", near_y)
    total = jnp.stack([mine, other])
    total = halving(total, x_index % 2 == 1, "x", near_x)
    total = halving(total, x_index >= 2, "x", far_x)

    conv = pl.pallas_call(
        conv_kernel,
        out_shape=jax.ShapeDtypeStruct((seq_count, 2 * positions), f32),
        scratch_shapes=rows + turned,
        name="conv",
        compiler_params=params,
        cost_estimate=cost,
    )(moved, filters, small_back, twiddle, *tables)
    signals = pl.pallas_call(
        back_kernel,
        out_shape=jax.ShapeDtypeStruct((seq_count, 1, 4 * positions), f32),
        scratch_shapes=rows + turned,
        name="back",
        compiler_params=params,
        cost_estimate=cost,
    )(conv, spec, filters, small_back, twiddle, *tables)
    returned = lax.all_to_all(signals, SEQ, split_axis=0, concat_axis=0, tiled=True)
    returned = returned.reshape(seq_count, 4 * positions)

    ordered = jnp.where(odd, total[::-1], total)
    rows_out = [jnp.where(upper_zhi, ordered[:, 1 - n], ordered[:, n]) for n in range(2)]
    ends = [
        lax.ppermute(rows_out[number], everyone, [(b, a) for a, b in pairs[number]])
        for number in range(2)
    ]
    grad_filter = (
        (ends[0] + ends[1])
        .reshape(2, 2, per_seq, positions)
        .transpose(1, 0, 2, 3)
        .reshape(2, 2 * per_seq, positions)
    )

    scale = 1.0 / math.sqrt(seq_count * positions)
    conv = returned[:, : per_seq * positions].reshape(1, channels, positions) * scale
    backward = returned[:, per_seq * positions :].reshape(1, channels, positions) * scale
    grad_gate = (grad_out.astype(f32) * conv).astype(bf16)
    return (backward.astype(bf16), grad_gate, grad_filter)


def solution(mesh):
    split = Mesh(mesh.devices.reshape(2, 4, 2, 8, 4), DP + SEQ)
    return jax.shard_map(
        step,
        mesh=split,
        in_specs=(P(DP, None, SEQ), P(DP, None, SEQ), P(DP, None, None, SEQ), P(None, DP, SEQ)),
        out_specs=(P(DP, None, SEQ), P(DP, None, SEQ), P(None, DP, SEQ)),
        check_vma=False,
    )
```

```python
import functools
import math

import jax
import jax.numpy as jnp
import numpy as np
from jax import lax
from jax.experimental import pallas as pl
from jax.experimental.pallas import tpu as pltpu
from jax.sharding import Mesh, PartitionSpec as P


f32 = jnp.float32
bf16 = jnp.bfloat16
SEQ = ("zlo", "y")
DP = ("zhi", "x", "core")
MIB = 1024 * 1024


def unit_roots(rows, columns, period):
    product = np.outer(np.arange(rows, dtype=np.int64), np.arange(columns, dtype=np.int64))
    angle = (product % period).astype(np.float64) * (2.0 * np.pi / period)
    return np.cos(angle).astype(np.float32), np.sin(angle).astype(np.float32)


def halves(values):
    high = values.astype(bf16)
    return high, (values - high.astype(f32)).astype(bf16)


def three_terms(values, axis):
    high, low = halves(values)
    return jnp.concatenate([high, low, high], axis=axis)


def small_table(points, inverse):
    cosine, sine = unit_roots(points, points, points)
    whole = np.concatenate([cosine, -sine], axis=1 if inverse else 0)
    high = whole.astype(bf16)
    low = (whole - high.astype(np.float32)).astype(bf16)
    return jnp.asarray(np.concatenate([high, high, low], axis=1))


def dot16(left, right):
    return jnp.dot(left, right, preferred_element_type=f32)


def tables_kernel(coarse_ref, fine_ref, cos_hi, cos_lo, sin_hi, sin_lo):
    steps = fine_ref.shape[1]

    @pl.loop(0, coarse_ref.shape[1])
    def _(a):
        at = pl.ds(pl.multiple_of(a * steps, steps), steps)
        coarse_cos, coarse_sin = coarse_ref[0, pl.ds(a, 1), :], coarse_ref[1, pl.ds(a, 1), :]
        fine_cos, fine_sin = fine_ref[0], fine_ref[1]
        cosine = coarse_cos * fine_cos - coarse_sin * fine_sin
        sine = coarse_sin * fine_cos + coarse_cos * fine_sin
        cos_hi[at, :], cos_lo[at, :] = halves(cosine)
        sin_hi[at, :], sin_lo[at, :] = halves(sine)


def root_tables(points):
    steps, columns = 32, points // 4
    coarse = jnp.asarray(np.stack(unit_roots(points // steps, columns, points // steps)))
    fine = jnp.asarray(np.stack(unit_roots(steps, columns, points)))
    return pl.pallas_call(
        tables_kernel,
        out_shape=[jax.ShapeDtypeStruct((points, columns), bf16)] * 4,
        name="root_tables",
        compiler_params=pltpu.CompilerParams(vmem_limit_bytes=16 * MIB),
        cost_estimate=pl.CostEstimate(
            flops=20 * points * columns, bytes_accessed=8 * points * columns, transcendentals=0
        ),
    )(coarse, fine)


def keep_quarters(rows_ref, place, count, real, imag, conjugate):
    rows, points = real.shape
    lane = lax.broadcasted_iota(jnp.int32, (1, points), 1)
    odd = lane % 2 == 1
    alternate = jnp.where(odd, -1.0, 1.0)
    early = jnp.where(lane % 4 < 2, 1.0, -1.0)
    outer = jnp.where((lane + 1) % 4 < 2, 1.0, -1.0)
    swap_real, swap_imag = jnp.where(odd, imag, real), jnp.where(odd, real, imag)
    turned = [
        (real, imag),
        (swap_real * outer, swap_imag * early),
        (real * alternate, imag * alternate),
        (swap_real * early, swap_imag * outer),
    ]
    if conjugate:
        turned[1], turned[3] = turned[3], turned[1]
    for m in range(4):
        for part, values in enumerate(turned[m]):
            high, low = halves(values)
            first = (part * count + place) * rows
            rows_ref[m, first : first + rows, :] = high
            rows_ref[m, 2 * count * rows + first : 2 * count * rows + first + rows, :] = low


def root_product(high_low, hi_ref, lo_ref):
    rows = high_low.shape[0] // 2
    both = dot16(high_low, hi_ref[...])
    return both[:rows] + both[rows:] + dot16(high_low[:rows], lo_ref[...])


def pack_kernel(
    out_hbm, gate_hbm, spec_hbm, packed_ref, out_ref, gate_ref, spec_ref, rows_ref, semaphores
):
    copies = [
        pltpu.make_async_copy(spec_hbm.at[0, 0], spec_ref.at[0], semaphores.at[0]),
        pltpu.make_async_copy(spec_hbm.at[0, 1], spec_ref.at[1], semaphores.at[1]),
        pltpu.make_async_copy(out_hbm.at[0], out_ref, semaphores.at[2]),
        pltpu.make_async_copy(gate_hbm.at[0], gate_ref, semaphores.at[3]),
    ]
    for copy in copies:
        copy.start()
    points = out_ref.shape[1]
    count = packed_ref.shape[0]
    for source in range(3):
        copies[source].wait()
        if source == 2:
            copies[3].wait()
        for start in range(0, points, 128):
            cut = slice(start, start + 128)
            slot = source * (points // 128) + start // 128
            if source == 2:
                rows_ref[slot] = out_ref[:, cut].astype(f32) * gate_ref[:, cut].astype(f32)
            else:
                rows_ref[slot] = spec_ref[source, :, cut]
            for channel in range(2):
                at = (2 * source + channel) * points + start
                packed_ref[:, 0, at : at + 128] = rows_ref[slot, pl.ds(channel, count, stride=2), :]


def finish_kernel(scale, returned_ref, out_ref, input_grad_ref, gate_grad_ref, rows_ref):
    points = out_ref.shape[2]
    count = returned_ref.shape[0]
    for source in range(2):
        for start in range(0, points, 128):
            cut = slice(start, start + 128)
            slot = source * (points // 128) + start // 128
            for channel in range(2):
                at = (2 * source + channel) * points + start
                rows_ref[slot, pl.ds(channel, count, stride=2), :] = returned_ref[:, 0, at : at + 128]
            values = rows_ref[slot] * scale
            if source == 0:
                gate_grad_ref[0, :, cut] = (out_ref[0, :, cut].astype(f32) * values).astype(bf16)
            else:
                input_grad_ref[0, :, cut] = values.astype(bf16)


def forward_kernel(
    core_ref, moved_ref, small_ref, twiddle_ref, cos_hi, cos_lo, sin_hi, sin_lo, spec_ref, kept_ref,
    away_ref, rows_ref,
):
    classes = moved_ref.shape[0]
    points = cos_hi.shape[0]
    scale = 1.0 / math.sqrt(classes * points)
    upper_core = core_ref[0] == 1
    quarter = classes // 4
    tw_cos, tw_sin = twiddle_ref[0] * scale, twiddle_ref[1] * scale
    for channel in range(2):
        delta = moved_ref[:, (4 + channel) * points : (5 + channel) * points]
        part = dot16(small_ref[...], three_terms(delta, 0))
        part_real, part_imag = part[:classes], part[classes:]
        turned_real = part_real * tw_cos + part_imag * tw_sin
        turned_imag = part_imag * tw_cos - part_real * tw_sin
        keep_quarters(rows_ref, channel, 2, turned_real, turned_imag, True)
    half = 2 * classes
    width = points // 4
    for tile in range(4):
        at = slice(tile * width, (tile + 1) * width)
        by_cos = root_product(rows_ref[tile], cos_hi, cos_lo)
        by_sin = root_product(rows_ref[tile], sin_hi, sin_lo)
        real = by_cos[:half] + by_sin[half:]
        imag = by_cos[half:] - by_sin[:half]
        for channel in range(2):
            mine = slice(channel * classes, (channel + 1) * classes)
            put_real = slice(channel * points + at.start, channel * points + at.stop)
            put_imag = slice((2 + channel) * points + at.start, (2 + channel) * points + at.stop)
            in_real, in_imag = moved_ref[:, put_real], moved_ref[:, put_imag]
            spec_ref[:, put_real] = real[mine]
            spec_ref[:, put_imag] = imag[mine]
            term_real = in_real * real[mine] + in_imag * imag[mine]
            term_imag = in_real * imag[mine] - in_imag * real[mine]
            for put, term in ((put_real, term_real), (put_imag, term_imag)):
                for side in range(2):
                    lower = term[2 * side * quarter : (2 * side + 1) * quarter]
                    upper = term[(2 * side + 1) * quarter : (2 * side + 2) * quarter]
                    kept_ref[side, :, put] = jnp.where(upper_core, upper, lower)
                    away_ref[side, :, put] = jnp.where(upper_core, lower, upper)


def inverse_rows(
    sign, first_ref, filt_ref, small_ref, twiddle_ref, tables, rows_ref, turned_ref
):
    cos_hi, cos_lo, sin_hi, sin_lo = tables
    classes = first_ref.shape[0]
    points = cos_hi.shape[0]
    for channel in range(2):
        real_at = slice(channel * points, (channel + 1) * points)
        imag_at = slice((2 + channel) * points, (3 + channel) * points)
        filt_real, filt_imag = filt_ref[:, real_at], filt_ref[:, imag_at] * sign
        first_real, first_imag = first_ref[:, real_at], first_ref[:, imag_at]
        keep_quarters(
            rows_ref,
            channel,
            2,
            first_real * filt_real - first_imag * filt_imag,
            first_real * filt_imag + first_imag * filt_real,
            False,
        )
    half = 2 * classes
    width = points // 4
    for tile in range(4):
        at = slice(tile * width, (tile + 1) * width)
        by_cos = root_product(rows_ref[tile], cos_hi, cos_lo)
        by_sin = root_product(rows_ref[tile], sin_hi, sin_lo)
        real = by_cos[:half] - by_sin[half:]
        imag = by_cos[half:] + by_sin[:half]
        tw_cos, tw_sin = twiddle_ref[0, :, at], twiddle_ref[1, :, at]
        for channel in range(2):
            mine = slice(channel * classes, (channel + 1) * classes)
            put = slice(channel * points + at.start, channel * points + at.stop)
            for part, turned in (
                (0, real[mine] * tw_cos - imag[mine] * tw_sin),
                (1, imag[mine] * tw_cos + real[mine] * tw_sin),
            ):
                high, low = halves(turned)
                for place, values in ((part, high), (2 + part, low), (4 + part, high)):
                    turned_ref[place * classes : (place + 1) * classes, put] = values
    return dot16(small_ref[...], turned_ref[...])


def conv_kernel(
    moved_ref, filt_ref, small_ref, twiddle_ref, cos_hi, cos_lo, sin_hi, sin_lo, conv_ref, rows_ref,
    turned_ref,
):
    tables = (cos_hi, cos_lo, sin_hi, sin_lo)
    conv_ref[...] = inverse_rows(
        1.0, moved_ref, filt_ref, small_ref, twiddle_ref, tables, rows_ref, turned_ref
    )


def back_kernel(
    conv_ref, spec_ref, filt_ref, small_ref, twiddle_ref, cos_hi, cos_lo, sin_hi, sin_lo, packed_ref,
    rows_ref, turned_ref,
):
    tables = (cos_hi, cos_lo, sin_hi, sin_lo)
    width = conv_ref.shape[1]
    packed_ref[:, 0, :width] = conv_ref[...]
    packed_ref[:, 0, width:] = inverse_rows(
        -1.0, spec_ref, filt_ref, small_ref, twiddle_ref, tables, rows_ref, turned_ref
    )


def staging_pairs(x_count, core_count, seq_count):
    pairs = []
    for number in range(2):
        found = []
        for d in range(2 * x_count * core_count):
            for s in range(seq_count):
                e0, core, near, far, e1 = [s >> bit & 1 for bit in (4, 3, 2, 1, 0)]
                row = ((e1 ^ number) * x_count + 2 * far + near) * core_count + core
                found.append((d * seq_count + s, row * seq_count + 2 * d + e0))
        pairs.append(found)
    return pairs


def kept_and_away(values, upper):
    half = values.shape[1] // 2
    lower, higher = values[:, :half], values[:, half:]
    return jnp.where(upper, higher, lower), jnp.where(upper, lower, higher)


def halving(values, upper, axis, pairs):
    kept, away = kept_and_away(values, upper)
    return kept + lax.ppermute(away, axis, pairs)


def doubling(values, upper, axis, pairs):
    other = lax.ppermute(values, axis, pairs)
    return jnp.concatenate(
        [jnp.where(upper, other, values), jnp.where(upper, values, other)], axis=1
    )


def step(grad_out, gate, input_spectrum, filter_spectrum):
    _, channels, positions = grad_out.shape
    seq_count = lax.axis_size(SEQ)
    x_count = lax.axis_size("x")
    everyone = DP + SEQ
    odd = lax.axis_index(SEQ) % 2 == 1
    upper_zhi = lax.axis_index("zhi") == 1
    upper_core = lax.axis_index("core") == 1
    x_index = lax.axis_index("x")
    pairs = staging_pairs(x_count, 2, seq_count)
    per_seq = channels // seq_count

    params = pltpu.CompilerParams(vmem_limit_bytes=16 * MIB)
    packed = pl.pallas_call(
        pack_kernel,
        out_shape=jax.ShapeDtypeStruct((seq_count, 1, 3 * per_seq * positions), f32),
        in_specs=[pl.BlockSpec(memory_space=pltpu.HBM)] * 3,
        scratch_shapes=[
            pltpu.VMEM((channels, positions), bf16),
            pltpu.VMEM((channels, positions), bf16),
            pltpu.VMEM((2, channels, positions), f32),
            pltpu.VMEM((3 * positions // 128, channels, 128), f32),
            pltpu.SemaphoreType.DMA((4,)),
        ],
        name="pack",
        compiler_params=pltpu.CompilerParams(vmem_limit_bytes=63 * MIB),
        cost_estimate=pl.CostEstimate(flops=10**5, bytes_accessed=2 * 10**6, transcendentals=0),
    )(grad_out, gate, input_spectrum)
    moved = lax.all_to_all(packed, SEQ, split_axis=0, concat_axis=0, tiled=True)
    moved = moved.reshape(seq_count, 3 * per_seq * positions)

    near_x = [(x, x ^ 1) for x in range(x_count)]
    far_x = [(x, x ^ 2) for x in range(x_count)]
    near_y = [(y, y ^ 1) for y in range(lax.axis_size("y"))]
    cores = [(0, 1), (1, 0)]
    half_row = 4 * positions
    got = [lax.ppermute(filter_spectrum, everyone, pairs[number]) for number in range(2)]
    ordered = [jnp.where(upper_zhi, got[1 - n], got[n]) for n in range(2)]
    mine = jnp.stack([jnp.where(odd, v[:, per_seq:], v[:, :per_seq]) for v in ordered])
    away = jnp.stack([jnp.where(odd, v[:, :per_seq], v[:, per_seq:]) for v in ordered])
    other = lax.ppermute(away, "y", near_y)
    mine, other = mine.reshape(2, half_row), other.reshape(2, half_row)
    filters = jnp.stack([jnp.where(odd, other, mine), jnp.where(odd, mine, other)])
    filters = doubling(filters, x_index >= 2, "x", far_x)
    filters = doubling(filters, x_index % 2 == 1, "x", near_x)
    filters = doubling(filters, upper_core, "core", cores).reshape(seq_count, half_row)

    tables = root_tables(positions)
    small_out = small_table(seq_count, False)
    small_back = small_table(seq_count, True)
    twiddle = jnp.asarray(np.stack(unit_roots(seq_count, positions, seq_count * positions)))

    core_flag = upper_core.astype(jnp.int32).reshape(1)
    wide = jax.ShapeDtypeStruct((seq_count, half_row), f32)
    part = jax.ShapeDtypeStruct((2, seq_count // 4, half_row), f32)
    rows = [pltpu.VMEM((4, 8 * seq_count, positions), bf16)]
    turned = [pltpu.VMEM((6 * seq_count, 2 * positions), bf16)]
    cost = pl.CostEstimate(flops=2 * 10**9, bytes_accessed=10**7, transcendentals=0)

    vmem = pl.BlockSpec(memory_space=pltpu.VMEM)
    spec, kept, away = pl.pallas_call(
        forward_kernel,
        out_shape=[wide, part, part],
        in_specs=[pl.BlockSpec(memory_space=pltpu.SMEM)] + [vmem] * 7,
        scratch_shapes=rows,
        name="forward",
        compiler_params=params,
        cost_estimate=cost,
    )(core_flag, moved, small_out, twiddle, *tables)

    total = kept + lax.ppermute(away, "core", cores)
    total = halving(total, x_index % 2 == 1, "x", near_x)
    total = halving(total, x_index >= 2, "x", far_x)
    mine = jnp.where(odd, total[1], total[0])
    other = lax.ppermute(jnp.where(odd, total[0], total[1]), "y", near_y)

    conv = pl.pallas_call(
        conv_kernel,
        out_shape=jax.ShapeDtypeStruct((seq_count, 2 * positions), f32),
        scratch_shapes=rows + turned,
        name="conv",
        compiler_params=params,
        cost_estimate=cost,
    )(moved, filters, small_back, twiddle, *tables)
    signals = pl.pallas_call(
        back_kernel,
        out_shape=jax.ShapeDtypeStruct((seq_count, 1, 4 * positions), f32),
        scratch_shapes=rows + turned,
        name="back",
        compiler_params=params,
        cost_estimate=cost,
    )(conv, spec, filters, small_back, twiddle, *tables)
    returned = lax.all_to_all(signals, SEQ, split_axis=0, concat_axis=0, tiled=True)

    ordered = jnp.stack([jnp.where(odd, other, mine), jnp.where(odd, mine, other)])
    rows_out = [jnp.where(upper_zhi, ordered[:, 1 - n], ordered[:, n]) for n in range(2)]
    ends = [
        lax.ppermute(rows_out[number], everyone, [(b, a) for a, b in pairs[number]])
        for number in range(2)
    ]
    grad_filter = (
        (ends[0] + ends[1])
        .reshape(2, 2, per_seq, positions)
        .transpose(1, 0, 2, 3)
        .reshape(2, 2 * per_seq, positions)
    )

    scale = 1.0 / math.sqrt(seq_count * positions)
    grad_input, grad_gate = pl.pallas_call(
        functools.partial(finish_kernel, scale),
        out_shape=[jax.ShapeDtypeStruct((1, channels, positions), bf16)] * 2,
        scratch_shapes=[pltpu.VMEM((2 * positions // 128, channels, 128), f32)],
        name="finish",
        compiler_params=params,
        cost_estimate=pl.CostEstimate(flops=10**5, bytes_accessed=2 * 10**6, transcendentals=0),
    )(returned, grad_out)
    return (grad_input, grad_gate, grad_filter)


def solution(mesh):
    split = Mesh(mesh.devices.reshape(2, 4, 2, 8, 4), DP + SEQ)
    return jax.shard_map(
        step,
        mesh=split,
        in_specs=(P(DP, None, SEQ), P(DP, None, SEQ), P(DP, None, None, SEQ), P(None, DP, SEQ)),
        out_specs=(P(DP, None, SEQ), P(DP, None, SEQ), P(None, DP, SEQ)),
        check_vma=False,
    )
```
